32 devices in a mesh: section: 16 (over z, y, x), tensor: 2 (over core).
Axes of the slice: x: 2, y: 2, z: 4, core: 2. Of those that a mesh axis runs over, the one named last changes fastest.
Arguments:
- embedded: bfloat16 [256, 4096], P(None, 'tensor'), may hold values from -6 to 6
- outbox: bfloat16 [16, 256, 4096], P('section', None, 'tensor'), may hold values from -6 to 6
- loss_grad: bfloat16 [256, 4096], P(None, 'tensor'), may hold values from -6 to 6
- grad_outbox: bfloat16 [16, 256, 4096], P('section', None, 'tensor'), may hold values from -6 to 6
- stash_held: bfloat16 [16, 256, 4096], P('section', None, 'tensor'), may hold values from -6 to 6
- norm_gain: bfloat16 [16, 4096], P('section', 'tensor'), may hold values from 0.099609375 to 1.8984375
- w_query: bfloat16 [16, 4096, 1024], P('section', None, 'tensor'), may hold values from -4 to 4
- w_keyval: bfloat16 [16, 4096, 512], P('section', None, 'tensor'), may hold values from -1 to 1
- w_out: bfloat16 [16, 1024, 4096], P('section', 'tensor'), may hold values from -0.25 to 0.25
Outputs:
- section_out: bfloat16 [16, 256, 4096], P('section', None, 'tensor')
- evicted: bfloat16 [16, 256, 4096], P('section', None, 'tensor')
- input_grad: bfloat16 [16, 256, 4096], P('section', None, 'tensor')
The draws below stay inside these ranges and needn't reach their ends.
All inputs are finite; a program needn't handle non-finite values.
Results may differ from the reference program's by a relative error of at most 0.013.
Values may be sent and summed in bfloat16 or wider, within the bound.
No kernel may reach another device: no remote copies, remote signals or barrier semaphores. Data moves between devices by JAX's collectives and lax.ppermute only.
A program may use at most 64 MiB of HBM per device.

```python
import jax
import jax.numpy as jnp
from jax import lax

D = 4096
HEAD = 128
HEADS_DEV = 4
SEQ = 256
QCOLS = 1024
N_SECTION = 16
N_TENSOR = 2


def keyval_helper(key):
    base = jax.random.fold_in(key, 7)
    table = jax.random.normal(base, (N_SECTION, D, 2 * HEAD * N_TENSOR), jnp.float32) * D ** (-0.5)
    return jnp.clip(table, -1.0, 1.0)


def draw_w_keyval(key, part):
    return keyval_helper(key).astype(jnp.bfloat16)


def draw_w_query(key, part):
    noise_key = jax.random.fold_in(key, 11)
    noise = jax.random.normal(noise_key, (N_SECTION, D, N_TENSOR * HEADS_DEV * HEAD), jnp.float32) * D ** (-0.5)
    values = noise
    return jnp.clip(values, -4.0, 4.0).astype(jnp.bfloat16)


def spiked(drawn, rng, source, target, shards_of, factor):
    def block_of(dim):
        return (jnp.arange(drawn.shape[dim]) // (drawn.shape[dim] // shards_of)).reshape((-1,) + (1,) * (drawn.ndim - 1 - dim))

    near = jax.random.permutation(rng, shards_of)[block_of(target)]
    other_side = (block_of(target) + shards_of // 2) % shards_of
    return jnp.where((block_of(source) == near) | (block_of(source) == other_side), factor * drawn, drawn)


def steps_of(rng, dims, cuts, smallest, largest):
    def one(position, shards_of):
        draws = jax.random.uniform(jax.random.fold_in(jax.random.fold_in(rng, 6), position), (shards_of,), jnp.float32, smallest / len(cuts), largest / len(cuts))
        return jnp.repeat(jnp.exp(draws), dims[position] // shards_of).reshape((-1,) + (1,) * (len(dims) - position - 1))

    level = one(*cuts[0])
    for cut in cuts[1:]:
        level = level * one(*cut)
    return level


def scatter_about(stream_key, dims, spread, reach, split=(), kind=jnp.bfloat16):
    values = jax.random.normal(stream_key, dims, jnp.float32) * spread
    if len(split) > 0:
        values = steps_of(stream_key, dims, split, -0.22, 0.18) * values
    return jnp.clip(values, min=-reach, max=reach).astype(kind)


def noise_with(key, shape, width, reach, shards, heavy, held_as=jnp.bfloat16):
    entries = width * jax.random.normal(key, shape, jnp.float32)
    if shards:
        entries = entries * steps_of(key, shape, shards, -0.22, 0.18)
    return jnp.clip(spiked(entries, jax.random.fold_in(key, 3), *heavy), -reach, reach).astype(held_as)


def setup_inputs(seed: int = 0) -> dict:
    splits = jax.random.split(jax.random.key(seed), 10)
    return {
        "embedded": scatter_about(splits[0], (SEQ, D), 1.0, 6.0, ((1, 2),)),
        "outbox": scatter_about(splits[1], (N_SECTION, SEQ, D), 1.0, 6.0, ((0, 16), (2, 2))),
        "loss_grad": scatter_about(splits[2], (SEQ, D), 1.0, 6.0, ((1, 2),)),
        "grad_outbox": scatter_about(splits[3], (N_SECTION, SEQ, D), 1.0, 6.0, ((0, 16), (2, 2))),
        "stash_held": scatter_about(splits[4], (N_SECTION, SEQ, D), 1.0, 6.0, ((0, 16), (2, 2))),
        "norm_gain": jnp.clip(1.0 + 0.18 * jax.random.normal(splits[5], (N_SECTION, D), jnp.float32), 0.099609375, 1.8984375).astype(jnp.bfloat16),
        "w_query": draw_w_query(jax.random.fold_in(splits[9], 71), 0),
        "w_keyval": draw_w_keyval(jax.random.fold_in(splits[9], 71), 0),
        "w_out": noise_with(splits[8], (N_SECTION, QCOLS, D), QCOLS ** -0.5, 0.25, ((0, 16), (1, 2)), (1, 2, 2, 2.0)),
    }


EPS = 1e-05

def norm_project(x, gain, w_query, w_keyval):
    xf = x.astype(jnp.float32)
    inv = lax.rsqrt(lax.optimization_barrier(jnp.mean(xf * xf, axis=-1, keepdims=True)) + EPS)
    normed = (xf * inv * gain.astype(jnp.float32)).astype(jnp.bfloat16)
    query = jnp.dot(normed, w_query, preferred_element_type=jnp.float32).astype(jnp.bfloat16)
    keyval = jnp.dot(normed, w_keyval, preferred_element_type=jnp.float32).astype(jnp.bfloat16)
    return (inv, query, keyval)

def attend(query, keyval):
    seq = query.shape[0]
    heads = query.reshape(seq, N_TENSOR, HEADS_DEV, HEAD).astype(jnp.float32)
    pairs = keyval.reshape(seq, N_TENSOR, 2, HEAD).astype(jnp.float32)
    keys = pairs[:, :, 0]
    values = pairs[:, :, 1]
    scores = jnp.einsum('sghd,tgd->ghst', heads, keys) * HEAD ** (-0.5)
    rows = lax.broadcasted_iota(jnp.int32, (seq, seq), 0)
    cols = lax.broadcasted_iota(jnp.int32, (seq, seq), 1)
    scores = jnp.where(rows >= cols, scores, -1e+30)
    top = lax.optimization_barrier(jnp.max(scores, axis=-1, keepdims=True))
    weights = jnp.exp(scores - top)
    prob = weights / lax.optimization_barrier(jnp.sum(weights, axis=-1, keepdims=True))
    prob_low = prob.astype(jnp.bfloat16)
    attn = jnp.einsum('ghst,tgd->sghd', prob_low.astype(jnp.float32), values).astype(jnp.bfloat16)
    return (prob, prob_low, heads, keys, values, attn.reshape(seq, -1))

def section_forward(x, gain, w_query, w_keyval, w_out):
    seq = x.shape[0]
    inv, query, keyval = norm_project(x, gain, w_query, w_keyval)
    attn = attend(query, keyval)[5]
    parts = jnp.einsum('sgc,gcd->gsd', attn.reshape(seq, N_TENSOR, -1).astype(jnp.float32), w_out.reshape(N_TENSOR, -1, D).astype(jnp.float32))
    parts = lax.optimization_barrier(parts.astype(jnp.bfloat16)).astype(jnp.float32)
    mixed = lax.optimization_barrier(jnp.sum(parts, axis=0))
    return (x.astype(jnp.float32) + mixed).astype(jnp.bfloat16)

def section_backward(x, grad, gain, w_query, w_keyval, w_out):
    seq = x.shape[0]
    inv, query, keyval = norm_project(x, gain, w_query, w_keyval)
    prob, prob_low, heads, keys, values, attn = attend(query, keyval)
    d_attn = jnp.dot(grad, w_out.T, preferred_element_type=jnp.float32).astype(jnp.bfloat16)
    d_heads = d_attn.reshape(seq, N_TENSOR, HEADS_DEV, HEAD).astype(jnp.float32)
    d_prob = jnp.einsum('sghd,tgd->ghst', d_heads, values)
    d_score = prob * (d_prob - lax.optimization_barrier(jnp.sum(prob * d_prob, axis=-1, keepdims=True))) * HEAD ** (-0.5)
    d_score = lax.optimization_barrier(d_score.astype(jnp.bfloat16)).astype(jnp.float32)
    d_query = jnp.einsum('ghst,tgd->sghd', d_score, keys).astype(jnp.bfloat16)
    d_key = jnp.einsum('ghst,sghd->tgd', d_score, heads).astype(jnp.bfloat16)
    d_value = jnp.einsum('ghst,sghd->tgd', prob_low.astype(jnp.float32), d_heads).astype(jnp.bfloat16)
    d_pairs = jnp.stack([d_key, d_value], axis=2)
    parts = jnp.einsum('sgc,dgc->gsd', d_query.reshape(seq, N_TENSOR, -1).astype(jnp.float32), w_query.reshape(D, N_TENSOR, -1).astype(jnp.float32))
    parts = parts + jnp.einsum('sgc,dgc->gsd', d_pairs.reshape(seq, N_TENSOR, -1).astype(jnp.float32), w_keyval.reshape(D, N_TENSOR, -1).astype(jnp.float32))
    parts = lax.optimization_barrier(parts.astype(jnp.bfloat16)).astype(jnp.float32)
    d_normed = lax.optimization_barrier(jnp.sum(parts, axis=0))
    scaled = d_normed * gain.astype(jnp.float32)
    xf = x.astype(jnp.float32)
    correction = lax.optimization_barrier(jnp.sum(scaled * xf, axis=-1, keepdims=True)) / D
    result = grad.astype(jnp.float32) + inv * scaled - xf * inv ** 3 * correction
    return result.astype(jnp.bfloat16)

def reference(embedded, outbox, loss_grad, grad_outbox, stash_held, norm_gain, w_query, w_keyval, w_out):
    inputs = jnp.concatenate([embedded[None], outbox[:-1]], axis=0)
    grads = jnp.concatenate([grad_outbox[1:], loss_grad[None]], axis=0)
    stashed = stash_held[::-1]

    def one_section(items):
        x, grad, stash, gain, wq, wkv, wo = items
        return (section_forward(x, gain, wq, wkv, wo), section_backward(stash, grad, gain, wq, wkv, wo))
    section_out, input_grad = lax.map(one_section, (inputs, grads, stashed, norm_gain, w_query, w_keyval, w_out))
    evicted = inputs[::-1]
    return (section_out, evicted, input_grad)
```

```python
import functools

import jax
import jax.numpy as jnp
from jax import lax
from jax.experimental import pallas as pl
from jax.experimental.pallas import tpu as pltpu
from jax.sharding import PartitionSpec as P

HEAD = 128
EPS = 1e-05
SCALE = HEAD ** (-0.5)
F32 = jnp.float32
BF16 = jnp.bfloat16


def rotate(value, axis, k):
    count = lax.axis_size(axis)
    return lax.ppermute(value, axis, [(i, (i - k) % count) for i in range(count)])


def gathered(value, axis):
    return [value] + [rotate(value, axis, k) for k in range(1, lax.axis_size(axis))]


def reduced(parts, axis):
    total = parts[0].astype(F32)
    for k in range(1, len(parts)):
        total = total + rotate(parts[k], axis, -k).astype(F32)
    return total


def nt(a, b):
    return lax.dot_general(a, b, (((1,), (1,)), ((), ())), preferred_element_type=F32)


def tn(a, b):
    return lax.dot_general(a, b, (((0,), (0,)), ((), ())), preferred_element_type=F32)


def nn(a, b):
    return jnp.dot(a, b, preferred_element_type=F32)


def vmem_spec():
    return pl.BlockSpec(memory_space=pltpu.VMEM)


def any_spec():
    return pl.BlockSpec(memory_space=pl.ANY)


def load_rows(col, count, hbm, buf, sem):
    width = hbm.shape[0] // count
    copies = []
    for k in range(count):
        block = lax.rem(col + k, count)
        copies.append(
            pltpu.make_async_copy(
                hbm.at[pl.ds(pl.multiple_of(block * width, width), width), :],
                buf.at[pl.ds(k * width, width), :],
                sem.at[k],
            )
        )
    for copy in copies:
        copy.start()
    return copies


def load_columns(col, count, hbm, buf, sem):
    width = hbm.shape[1] // count
    copies = []
    for k in range(count):
        block = lax.rem(col + k, count)
        copies.append(
            pltpu.make_async_copy(
                hbm.at[:, pl.ds(pl.multiple_of(block * width, width), width)],
                buf.at[k],
                sem.at[k],
            )
        )
    for copy in copies:
        copy.start()
    return copies


def normalize(xs, gains, normed):
    width = xs[0].shape[1]
    total = None
    for x in xs:
        xf = x[...].astype(F32)
        part = jnp.sum(xf * xf, axis=-1, keepdims=True)
        total = part if total is None else total + part
    inv = lax.rsqrt(total / (width * len(xs)) + EPS)
    for k, x in enumerate(xs):
        xf = x[...].astype(F32)
        normed[:, k * width : (k + 1) * width] = (xf * inv * gains[k][...].astype(F32)).astype(BF16)
    return inv


def causal_mask(seq):
    rows = lax.broadcasted_iota(jnp.int32, (seq, seq), 0)
    cols = lax.broadcasted_iota(jnp.int32, (seq, seq), 1)
    return rows >= cols


def softmax(query, keys, mask):
    scores = jnp.where(mask, nt(query, keys) * SCALE, -1e30)
    top = jnp.max(scores, axis=-1, keepdims=True)
    weights = jnp.exp(scores - top)
    return weights / jnp.sum(weights, axis=-1, keepdims=True)


def forward_kernel(count, heads, *refs):
    xs, refs = refs[:count], refs[count:]
    gains, refs = refs[:count], refs[count:]
    wq_hbm, wkv_hbm, wo_hbm, refs = *refs[:3], refs[3:]
    outs, refs = refs[:count], refs[count:]
    normed, wq, wkv, wo, attn, sems = refs
    col = lax.axis_index("tensor")
    first = load_rows(col, count, wq_hbm, wq, sems.at[0])
    first += load_rows(col, count, wkv_hbm, wkv, sems.at[1])
    last = load_columns(col, count, wo_hbm, wo, sems.at[2])
    normalize(xs, gains, normed)
    for copy in first:
        copy.wait()
    keyval = nn(normed[...], wkv[...]).astype(BF16)
    query = nn(normed[...], wq[...]).astype(BF16)
    keys, values = keyval[:, :HEAD], keyval[:, HEAD:]
    mask = causal_mask(query.shape[0])
    for h in range(heads):
        prob = softmax(query[:, h * HEAD : (h + 1) * HEAD], keys, mask)
        attn[:, h * HEAD : (h + 1) * HEAD] = nn(prob.astype(BF16), values).astype(BF16)
    for k in reversed(range(count)):
        last[k].wait()
        outs[k][...] = nn(attn[...], wo[k]).astype(BF16)


def recompute_kernel(count, heads, *refs):
    xs, refs = refs[:count], refs[count:]
    gains, refs = refs[:count], refs[count:]
    wq_hbm, wkv_hbm, refs = *refs[:2], refs[2:]
    query_out, keyval_out, prob_out, inv_out, refs = *refs[:4], refs[4:]
    normed, wq, wkv, sems = refs
    col = lax.axis_index("tensor")
    first = load_rows(col, count, wq_hbm, wq, sems.at[0])
    first += load_rows(col, count, wkv_hbm, wkv, sems.at[1])
    inv = normalize(xs, gains, normed)
    inv_out[...] = jnp.broadcast_to(inv, inv_out.shape)
    for copy in first:
        copy.wait()
    keyval = nn(normed[...], wkv[...]).astype(BF16)
    query = nn(normed[...], wq[...]).astype(BF16)
    query_out[...] = query
    keyval_out[...] = keyval
    mask = causal_mask(query.shape[0])
    for h in range(heads):
        prob_out[h] = softmax(query[:, h * HEAD : (h + 1) * HEAD], keyval[:, :HEAD], mask)


def backward_kernel(count, heads, *refs):
    gs, refs = refs[:count], refs[count:]
    xs, refs = refs[:count], refs[count:]
    gains, refs = refs[:count], refs[count:]
    query, keyval, prob, wq_hbm, wkv_hbm, wo_hbm, refs = *refs[:6], refs[6:]
    outs, refs = refs[:count], refs[count:]
    total_out, refs = refs[0], refs[1:]
    wq, wkv, wo, d_query, sems = refs
    width = xs[0].shape[1]
    col = lax.axis_index("tensor")
    first = load_columns(col, count, wo_hbm, wo, sems.at[2])
    last = load_rows(col, count, wq_hbm, wq, sems.at[0])
    last += load_rows(col, count, wkv_hbm, wkv, sems.at[1])
    d_attn = None
    for k in range(count):
        first[k].wait()
        part = nt(gs[k][...], wo[k])
        d_attn = part if d_attn is None else d_attn + part
    d_attn = d_attn.astype(BF16)
    keys, values = keyval[:, :HEAD], keyval[:, HEAD:]
    d_key = d_value = None
    for h in range(heads):
        span = slice(h * HEAD, (h + 1) * HEAD)
        p = prob[h]
        d_head = d_attn[:, span]
        d_prob = nt(d_head, values)
        d_score = p * (d_prob - jnp.sum(p * d_prob, axis=-1, keepdims=True)) * SCALE
        d_score = d_score.astype(BF16)
        d_query[:, span] = nn(d_score, keys).astype(BF16)
        dk = tn(d_score, query[:, span])
        dv = tn(p.astype(BF16), d_head)
        d_key = dk if d_key is None else d_key + dk
        d_value = dv if d_value is None else d_value + dv
    d_pairs = jnp.concatenate([d_key.astype(BF16), d_value.astype(BF16)], axis=1)
    for copy in last:
        copy.wait()
    total = None
    for k in reversed(range(count)):
        rows = slice(k * width, (k + 1) * width)
        term = (nt(d_query[...], wq[rows, :]) + nt(d_pairs, wkv[rows, :])).astype(BF16)
        outs[k][...] = term
        scaled = term.astype(F32) * gains[k][...].astype(F32)
        part = jnp.sum(scaled * xs[k][...].astype(F32), axis=-1, keepdims=True)
        total = part if total is None else total + part
    total_out[...] = jnp.broadcast_to(total, total_out.shape)


def call(kernel, count, heads, name, ins, n_vmem, out_shape, scratch, flops, moved):
    return pl.pallas_call(
        functools.partial(kernel, count, heads),
        name=name,
        out_shape=out_shape,
        in_specs=[vmem_spec()] * n_vmem + [any_spec()] * (len(ins) - n_vmem),
        out_specs=[vmem_spec()] * len(out_shape),
        scratch_shapes=scratch,
        compiler_params=pltpu.CompilerParams(vmem_limit_bytes=48 * 2**20),
        cost_estimate=pl.CostEstimate(flops=flops, bytes_accessed=moved, transcendentals=0),
    )(*ins)


def local(
    embedded, outbox, loss_grad, grad_outbox, stash_held, norm_gain, w_query, w_keyval, w_out
):
    sections = lax.axis_size("section")
    count = lax.axis_size("tensor")
    position = lax.axis_index("section")
    held, grads_held, stash_held = outbox[0], grad_outbox[0], stash_held[0]
    seq, width = held.shape
    model = width * count
    wq, wkv, wo = w_query[0], w_keyval[0], w_out[0]
    qcols, kvcols = wq.shape[1], wkv.shape[1]
    heads = qcols // HEAD
    shape = jax.ShapeDtypeStruct

    up = [(s, s + 1) for s in range(sections - 1)]
    down = [(s + 1, s) for s in range(sections - 1)]
    mirror = [(s, sections - 1 - s) for s in range(sections)]
    evict = [(s, sections - 2 - s) for s in range(sections - 1)] + [(sections - 1, sections - 1)]

    arrived = lax.ppermute(held, "section", up)
    fetched = lax.ppermute(stash_held, "section", mirror)
    coming = lax.ppermute(grads_held, "section", down)
    leaving = jnp.where(position == sections - 1, embedded, held)
    leaving, fetched = lax.optimization_barrier((leaving, fetched))
    evicted = lax.ppermute(leaving, "section", evict)

    gains = gathered(norm_gain, "tensor")

    x_shard = jnp.where(position == 0, embedded, arrived)
    xs = gathered(x_shard, "tensor")
    weights = [
        pltpu.VMEM((model, qcols), BF16),
        pltpu.VMEM((model, kvcols), BF16),
    ]
    wo_buf = pltpu.VMEM((count, qcols, width), BF16)
    sems = pltpu.SemaphoreType.DMA((3, count))
    normed = pltpu.VMEM((seq, model), BF16)
    shares = [shape((seq, width), BF16)] * count
    proj = 2 * seq * model * (qcols + kvcols)
    out_flops = 2 * seq * model * qcols
    moved = 2 * model * (2 * qcols + kvcols)
    parts = call(
        forward_kernel, count, heads, "forward",
        [*xs, *gains, wq, wkv, wo], 2 * count, shares,
        [normed, *weights, wo_buf, pltpu.VMEM((seq, qcols), BF16), sems],
        proj + out_flops, moved,
    )
    mixed = reduced(parts, "tensor")
    section_out = (x_shard.astype(F32) + mixed).astype(BF16)

    bs = gathered(fetched, "tensor")
    query, keyval, prob, inv = call(
        recompute_kernel, count, heads, "recompute",
        [*bs, *gains, wq, wkv], 2 * count,
        [
            shape((seq, qcols), BF16),
            shape((seq, kvcols), BF16),
            shape((heads, seq, seq), F32),
            shape((seq, HEAD), F32),
        ],
        [normed, *weights, sems],
        proj, moved,
    )
    g_shard = jnp.where(position == sections - 1, loss_grad, coming)
    gs = gathered(g_shard, "tensor")
    *terms, total = call(
        backward_kernel, count, heads, "backward",
        [*gs, *bs, *gains, query, keyval, prob, wq, wkv, wo], 3 * count + 3,
        [*shares, shape((seq, HEAD), F32)],
        [*weights, wo_buf, pltpu.VMEM((seq, qcols), BF16), sems],
        proj + out_flops, moved,
    )
    d_normed = reduced(terms, "tensor")
    total = sum(gathered(total, "tensor"))[:, :1]
    inv = inv[:, :1]
    scaled = d_normed * norm_gain.astype(F32)
    result = (
        g_shard.astype(F32) + inv * scaled - fetched.astype(F32) * inv**3 * (total / model)
    )
    return section_out[None], evicted[None], result.astype(BF16)[None]


def solution(mesh):
    return jax.shard_map(
        local,
        mesh=mesh,
        in_specs=(
            P(None, "tensor"),
            P("section", None, "tensor"),
            P(None, "tensor"),
            P("section", None, "tensor"),
            P("section", None, "tensor"),
            P("section", "tensor"),
            P("section", None, "tensor"),
            P("section", None, "tensor"),
            P("section", "tensor", None),
        ),
        out_specs=(
            P("section", None, "tensor"),
            P("section", None, "tensor"),
            P("section", None, "tensor"),
        ),
        check_vma=False,
    )
```

```python
import functools

import jax
import jax.numpy as jnp
from jax import lax
from jax.experimental import pallas as pl
from jax.experimental.pallas import tpu as pltpu
from jax.sharding import PartitionSpec as P


HEAD = 128
EPS = 1e-05
SCALE = HEAD ** (-0.5)
F32 = jnp.float32
BF16 = jnp.bfloat16


def rotate(value, axis, k):
    count = lax.axis_size(axis)
    return lax.ppermute(value, axis, [(i, (i - k) % count) for i in range(count)])


def gathered(value, axis):
    return [value] + [rotate(value, axis, k) for k in range(1, lax.axis_size(axis))]


def reduced(parts, axis):
    total = parts[0].astype(F32)
    for k in range(1, len(parts)):
        total = total + rotate(parts[k], axis, -k).astype(F32)
    return total


def nt(a, b):
    return lax.dot_general(a, b, (((1,), (1,)), ((), ())), preferred_element_type=F32)


def tn(a, b):
    return lax.dot_general(a, b, (((0,), (0,)), ((), ())), preferred_element_type=F32)


def nn(a, b):
    return jnp.dot(a, b, preferred_element_type=F32)


def vmem_spec():
    return pl.BlockSpec(memory_space=pltpu.VMEM)


def any_spec():
    return pl.BlockSpec(memory_space=pl.ANY)


def load_rows(col, count, hbm, buf, sem):
    width = hbm.shape[0] // count
    copies = []
    for k in range(count):
        block = lax.rem(col + k, count)
        copies.append(
            pltpu.make_async_copy(
                hbm.at[pl.ds(pl.multiple_of(block * width, width), width), :],
                buf.at[pl.ds(k * width, width), :],
                sem.at[k],
            )
        )
    for copy in copies:
        copy.start()
    return copies


def load_columns(col, count, hbm, buf, sem):
    width = hbm.shape[1] // count
    copies = []
    for k in range(count):
        block = lax.rem(col + k, count)
        copies.append(
            pltpu.make_async_copy(
                hbm.at[:, pl.ds(pl.multiple_of(block * width, width), width)],
                buf.at[k],
                sem.at[k],
            )
        )
    for copy in copies:
        copy.start()
    return copies


def normalize(xs, gains, normed):
    width = xs[0].shape[1]
    total = None
    for x in xs:
        xf = x[...].astype(F32)
        part = jnp.sum(xf * xf, axis=-1, keepdims=True)
        total = part if total is None else total + part
    inv = lax.rsqrt(total / (width * len(xs)) + EPS)
    for k, x in enumerate(xs):
        xf = x[...].astype(F32)
        normed[:, k * width : (k + 1) * width] = (xf * inv * gains[k][...].astype(F32)).astype(BF16)
    return inv


def causal_mask(seq):
    rows = lax.broadcasted_iota(jnp.int32, (seq, seq), 0)
    cols = lax.broadcasted_iota(jnp.int32, (seq, seq), 1)
    return rows >= cols


def softmax(query, keys, mask):
    scores = jnp.where(mask, nt(query, keys) * SCALE, -1e30)
    top = jnp.max(scores, axis=-1, keepdims=True)
    weights = jnp.exp(scores - top)
    return weights / jnp.sum(weights, axis=-1, keepdims=True)


def forward_kernel(count, heads, *refs):
    xs, refs = refs[:count], refs[count:]
    gains, refs = refs[:count], refs[count:]
    wq_hbm, wkv_hbm, wo_hbm, refs = *refs[:3], refs[3:]
    outs, refs = refs[:count], refs[count:]
    normed, wq, wkv, wo, attn, sems = refs
    col = lax.axis_index("tensor")
    first = load_rows(col, count, wq_hbm, wq, sems.at[0])
    first += load_rows(col, count, wkv_hbm, wkv, sems.at[1])
    last = load_columns(col, count, wo_hbm, wo, sems.at[2])
    normalize(xs, gains, normed)
    for copy in first:
        copy.wait()
    keyval = nn(normed[...], wkv[...]).astype(BF16)
    query = nn(normed[...], wq[...]).astype(BF16)
    keys, values = keyval[:, :HEAD], keyval[:, HEAD:]
    mask = causal_mask(query.shape[0])
    for h in range(heads):
        prob = softmax(query[:, h * HEAD : (h + 1) * HEAD], keys, mask)
        attn[:, h * HEAD : (h + 1) * HEAD] = nn(prob.astype(BF16), values).astype(BF16)
    for k in reversed(range(count)):
        last[k].wait()
        outs[k][...] = nn(attn[...], wo[k]).astype(BF16)


def recompute_kernel(count, heads, *refs):
    xs, refs = refs[:count], refs[count:]
    gains, refs = refs[:count], refs[count:]
    wq_hbm, wkv_hbm, refs = *refs[:2], refs[2:]
    query_out, keyval_out, prob_out, inv_out, refs = *refs[:4], refs[4:]
    normed, wq, wkv, sems = refs
    col = lax.axis_index("tensor")
    first = load_rows(col, count, wq_hbm, wq, sems.at[0])
    first += load_rows(col, count, wkv_hbm, wkv, sems.at[1])
    inv = normalize(xs, gains, normed)
    inv_out[...] = jnp.broadcast_to(inv, inv_out.shape)
    for copy in first:
        copy.wait()
    keyval = nn(normed[...], wkv[...]).astype(BF16)
    query = nn(normed[...], wq[...]).astype(BF16)
    query_out[...] = query
    keyval_out[...] = keyval
    mask = causal_mask(query.shape[0])
    for h in range(heads):
        prob_out[h] = softmax(query[:, h * HEAD : (h + 1) * HEAD], keyval[:, :HEAD], mask)


def backward_kernel(count, heads, *refs):
    gs, refs = refs[:count], refs[count:]
    xs, refs = refs[:count], refs[count:]
    gains, refs = refs[:count], refs[count:]
    query, keyval, prob, wq_hbm, wkv_hbm, wo_hbm, refs = *refs[:6], refs[6:]
    outs, refs = refs[:count], refs[count:]
    total_out, refs = refs[0], refs[1:]
    wq, wkv, wo, d_query, sems = refs
    width = xs[0].shape[1]
    col = lax.axis_index("tensor")
    first = load_columns(col, count, wo_hbm, wo, sems.at[2])
    last = load_rows(col, count, wq_hbm, wq, sems.at[0])
    last += load_rows(col, count, wkv_hbm, wkv, sems.at[1])
    d_attn = None
    for k in range(count):
        first[k].wait()
        part = nt(gs[k][...], wo[k])
        d_attn = part if d_attn is None else d_attn + part
    d_attn = d_attn.astype(BF16)
    keys, values = keyval[:, :HEAD], keyval[:, HEAD:]
    d_key = d_value = None
    for h in range(heads):
        span = slice(h * HEAD, (h + 1) * HEAD)
        p = prob[h]
        d_head = d_attn[:, span]
        d_prob = nt(d_head, values)
        d_score = p * (d_prob - jnp.sum(p * d_prob, axis=-1, keepdims=True)) * SCALE
        d_score = d_score.astype(BF16)
        d_query[:, span] = nn(d_score, keys).astype(BF16)
        dk = tn(d_score, query[:, span])
        dv = tn(p.astype(BF16), d_head)
        d_key = dk if d_key is None else d_key + dk
        d_value = dv if d_value is None else d_value + dv
    d_pairs = jnp.concatenate([d_key.astype(BF16), d_value.astype(BF16)], axis=1)
    for copy in last:
        copy.wait()
    total = None
    for k in reversed(range(count)):
        rows = slice(k * width, (k + 1) * width)
        term = (nt(d_query[...], wq[rows, :]) + nt(d_pairs, wkv[rows, :])).astype(BF16)
        outs[k][...] = term
        scaled = term.astype(F32) * gains[k][...].astype(F32)
        part = jnp.sum(scaled * xs[k][...].astype(F32), axis=-1, keepdims=True)
        total = part if total is None else total + part
    total_out[...] = jnp.broadcast_to(total, total_out.shape)


def call(kernel, count, heads, ins, n_vmem, out_shape, scratch, flops, moved):
    return pl.pallas_call(
        functools.partial(kernel, count, heads),
        out_shape=out_shape,
        in_specs=[vmem_spec()] * n_vmem + [any_spec()] * (len(ins) - n_vmem),
        out_specs=[vmem_spec()] * len(out_shape),
        scratch_shapes=scratch,
        compiler_params=pltpu.CompilerParams(vmem_limit_bytes=48 * 2**20),
        cost_estimate=pl.CostEstimate(flops=flops, bytes_accessed=moved, transcendentals=0),
    )(*ins)


def local(
    embedded, outbox, loss_grad, grad_outbox, stash_held, norm_gain, w_query, w_keyval, w_out
):
    sections = lax.axis_size("section")
    count = lax.axis_size("tensor")
    position = lax.axis_index("section")
    held, grads_held, stash_held = outbox[0], grad_outbox[0], stash_held[0]
    seq, width = held.shape
    model = width * count
    wq, wkv, wo = w_query[0], w_keyval[0], w_out[0]
    qcols, kvcols = wq.shape[1], wkv.shape[1]
    heads = qcols // HEAD
    shape = jax.ShapeDtypeStruct

    block = sections // 4
    high = sections - block
    crossing = [s for s in range(sections - 1) if (s + 1) % block == 0]
    inside = [s for s in range(sections - 1) if (s + 1) % block]

    def send(value, pairs):
        return lax.ppermute(value, "section", pairs)

    arrived_inside = send(held, [(s, s + 1) for s in inside])
    arrived_crossing = send(held, [(s, s + 1) for s in crossing])
    fetched = send(stash_held, [(s, sections - 1 - s) for s in range(sections)])
    coming = send(grads_held, [(s + 1, s) for s in range(sections - 1)])
    evicted = send(held, [(s, sections - 2 - s) for s in range(high)])
    relayed = send(arrived_inside, [(s, sections - 1 - s) for s in range(high + 1, sections)])

    gains = gathered(norm_gain, "tensor")

    arrived = jnp.where(position % block == 0, arrived_crossing, arrived_inside)
    x_shard = jnp.where(position == 0, embedded, arrived)
    xs = gathered(x_shard, "tensor")
    weights = [
        pltpu.VMEM((model, qcols), BF16),
        pltpu.VMEM((model, kvcols), BF16),
    ]
    wo_buf = pltpu.VMEM((count, qcols, width), BF16)
    sems = pltpu.SemaphoreType.DMA((3, count))
    normed = pltpu.VMEM((seq, model), BF16)
    shares = [shape((seq, width), BF16)] * count
    proj = 2 * seq * model * (qcols + kvcols)
    out_flops = 2 * seq * model * qcols
    moved = 2 * model * (2 * qcols + kvcols)
    parts = call(
        forward_kernel, count, heads,
        [*xs, *gains, wq, wkv, wo], 2 * count, shares,
        [normed, *weights, wo_buf, pltpu.VMEM((seq, qcols), BF16), sems],
        proj + out_flops, moved,
    )
    mixed = reduced(parts, "tensor")
    section_out = (x_shard.astype(F32) + mixed).astype(BF16)

    bs = gathered(fetched, "tensor")
    query, keyval, prob, inv = call(
        recompute_kernel, count, heads,
        [*bs, *gains, wq, wkv], 2 * count,
        [
            shape((seq, qcols), BF16),
            shape((seq, kvcols), BF16),
            shape((heads, seq, seq), F32),
            shape((seq, HEAD), F32),
        ],
        [normed, *weights, sems],
        proj, moved,
    )
    g_shard = jnp.where(position == sections - 1, loss_grad, coming)
    gs = gathered(g_shard, "tensor")
    *terms, total = call(
        backward_kernel, count, heads,
        [*gs, *bs, *gains, query, keyval, prob, wq, wkv, wo], 3 * count + 3,
        [*shares, shape((seq, HEAD), F32)],
        [*weights, wo_buf, pltpu.VMEM((seq, qcols), BF16), sems],
        proj + out_flops, moved,
    )
    place, last, _ = lax.optimization_barrier((position, embedded, total))
    evicted = jnp.where(
        place < block - 1, relayed, jnp.where(place < sections - 1, evicted, last)
    )
    d_normed = reduced(terms, "tensor")
    total = sum(gathered(total, "tensor"))[:, :1]
    inv = inv[:, :1]
    scaled = d_normed * norm_gain.astype(F32)
    result = (
        g_shard.astype(F32) + inv * scaled - fetched.astype(F32) * inv**3 * (total / model)
    )
    return section_out[None], evicted[None], result.astype(BF16)[None]


def solution(mesh):
    return jax.shard_map(
        local,
        mesh=mesh,
        in_specs=(
            P(None, "tensor"),
            P("section", None, "tensor"),
            P(None, "tensor"),
            P("section", None, "tensor"),
            P("section", None, "tensor"),
            P("section", "tensor"),
            P("section", None, "tensor"),
            P("section", None, "tensor"),
            P("section", "tensor", None),
        ),
        out_specs=(
            P("section", None, "tensor"),
            P("section", None, "tensor"),
            P("section", None, "tensor"),
        ),
        check_vma=False,
    )
```

```python
import functools

import jax
import jax.numpy as jnp
from jax import lax
from jax.experimental import pallas as pl
from jax.experimental.pallas import tpu as pltpu
from jax.sharding import PartitionSpec as P


HEAD = 128
EPS = 1e-05
SCALE = HEAD ** (-0.5)
F32 = jnp.float32
BF16 = jnp.bfloat16

LIMIT = 14 * 2**20


def rotate(value, axis, k):
    count = lax.axis_size(axis)
    return lax.ppermute(value, axis, [(i, (i - k) % count) for i in range(count)])


def gathered(value, axis):
    return [value] + [rotate(value, axis, k) for k in range(1, lax.axis_size(axis))]


def reduced(parts, axis):
    total = parts[0].astype(F32)
    for k in range(1, len(parts)):
        total = total + rotate(parts[k], axis, -k).astype(F32)
    return total


def nt(a, b):
    return lax.dot_general(a, b, (((1,), (1,)), ((), ())), preferred_element_type=F32)


def tn(a, b):
    return lax.dot_general(a, b, (((0,), (0,)), ((), ())), preferred_element_type=F32)


def nn(a, b):
    return jnp.dot(a, b, preferred_element_type=F32)


def vmem_spec():
    return pl.BlockSpec(memory_space=pltpu.VMEM)


def rows_of(ref, col, k, count):
    width = ref.shape[0] // count
    return ref[pl.ds(pl.multiple_of(lax.rem(col + k, count) * width, width), width), :]


def columns_of(ref, col, k, count):
    width = ref.shape[1] // count
    return ref[:, pl.ds(pl.multiple_of(lax.rem(col + k, count) * width, width), width)]


def project(normed, weights, col, count):
    width = weights.shape[0] // count
    total = None
    for k in range(count):
        part = nn(normed[:, k * width : (k + 1) * width], rows_of(weights, col, k, count))
        total = part if total is None else total + part
    return total.astype(BF16)


def normalize(xs, gains, normed):
    width = xs[0].shape[1]
    total = None
    for x in xs:
        xf = x[...].astype(F32)
        part = jnp.sum(xf * xf, axis=-1, keepdims=True)
        total = part if total is None else total + part
    inv = lax.rsqrt(total / (width * len(xs)) + EPS)
    for k, x in enumerate(xs):
        xf = x[...].astype(F32)
        normed[:, k * width : (k + 1) * width] = (xf * inv * gains[k][...].astype(F32)).astype(BF16)
    return inv


def causal_mask(seq):
    rows = lax.broadcasted_iota(jnp.int32, (seq, seq), 0)
    cols = lax.broadcasted_iota(jnp.int32, (seq, seq), 1)
    return rows >= cols


def softmax(query, keys, mask):
    scores = jnp.where(mask, nt(query, keys) * SCALE, -1e30)
    top = jnp.max(scores, axis=-1, keepdims=True)
    weights = jnp.exp(scores - top)
    return weights / jnp.sum(weights, axis=-1, keepdims=True)


def forward_kernel(count, heads, *refs):
    xs, refs = refs[:count], refs[count:]
    gains, refs = refs[:count], refs[count:]
    wq, wkv, wo, refs = *refs[:3], refs[3:]
    outs, (normed, attn) = refs[:count], refs[count:]
    col = lax.axis_index("tensor")
    normalize(xs, gains, normed)
    keyval = project(normed, wkv, col, count)
    query = project(normed, wq, col, count)
    keys, values = keyval[:, :HEAD], keyval[:, HEAD:]
    mask = causal_mask(query.shape[0])
    for h in range(heads):
        prob = softmax(query[:, h * HEAD : (h + 1) * HEAD], keys, mask)
        attn[:, h * HEAD : (h + 1) * HEAD] = nn(prob.astype(BF16), values).astype(BF16)
    for k in reversed(range(count)):
        outs[k][...] = nn(attn[...], columns_of(wo, col, k, count)).astype(BF16)


def recompute_kernel(count, heads, *refs):
    xs, refs = refs[:count], refs[count:]
    gains, refs = refs[:count], refs[count:]
    wq, wkv, query_out, keyval_out, prob_out, inv_out, normed = refs
    col = lax.axis_index("tensor")
    inv = normalize(xs, gains, normed)
    inv_out[...] = jnp.broadcast_to(inv, inv_out.shape)
    keyval = project(normed, wkv, col, count)
    query = project(normed, wq, col, count)
    query_out[...] = query
    keyval_out[...] = keyval
    mask = causal_mask(query.shape[0])
    for h in range(heads):
        prob_out[h] = softmax(query[:, h * HEAD : (h + 1) * HEAD], keyval[:, :HEAD], mask)


def backward_kernel(count, heads, *refs):
    gs, refs = refs[:count], refs[count:]
    xs, refs = refs[:count], refs[count:]
    gains, refs = refs[:count], refs[count:]
    query, keyval, prob, wq, wkv, wo, refs = *refs[:6], refs[6:]
    outs, (total_out, d_query) = refs[:count], refs[count:]
    col = lax.axis_index("tensor")
    d_attn = None
    for k in range(count):
        part = nt(gs[k][...], columns_of(wo, col, k, count))
        d_attn = part if d_attn is None else d_attn + part
    d_attn = d_attn.astype(BF16)
    keys, values = keyval[:, :HEAD], keyval[:, HEAD:]
    d_key = d_value = None
    for h in range(heads):
        span = slice(h * HEAD, (h + 1) * HEAD)
        p = prob[h]
        d_head = d_attn[:, span]
        d_prob = nt(d_head, values)
        d_score = p * (d_prob - jnp.sum(p * d_prob, axis=-1, keepdims=True)) * SCALE
        d_score = d_score.astype(BF16)
        d_query[:, span] = nn(d_score, keys).astype(BF16)
        dk = tn(d_score, query[:, span])
        dv = tn(p.astype(BF16), d_head)
        d_key = dk if d_key is None else d_key + dk
        d_value = dv if d_value is None else d_value + dv
    d_pairs = jnp.concatenate([d_key.astype(BF16), d_value.astype(BF16)], axis=1)
    total = None
    for k in reversed(range(count)):
        term = nt(d_query[...], rows_of(wq, col, k, count))
        term = (term + nt(d_pairs, rows_of(wkv, col, k, count))).astype(BF16)
        outs[k][...] = term
        scaled = term.astype(F32) * gains[k][...].astype(F32)
        part = jnp.sum(scaled * xs[k][...].astype(F32), axis=-1, keepdims=True)
        total = part if total is None else total + part
    total_out[...] = jnp.broadcast_to(total, total_out.shape)


def call(kernel, count, heads, ins, out_shape, scratch, flops, moved):
    return pl.pallas_call(
        functools.partial(kernel, count, heads),
        out_shape=out_shape,
        in_specs=[vmem_spec()] * len(ins),
        out_specs=[vmem_spec()] * len(out_shape),
        scratch_shapes=scratch,
        compiler_params=pltpu.CompilerParams(vmem_limit_bytes=LIMIT),
        cost_estimate=pl.CostEstimate(flops=flops, bytes_accessed=moved, transcendentals=0),
    )(*ins)


def local(
    embedded, outbox, loss_grad, grad_outbox, stash_held, norm_gain, w_query, w_keyval, w_out
):
    sections = lax.axis_size("section")
    count = lax.axis_size("tensor")
    position = lax.axis_index("section")
    held, grads_held, stash_held = outbox[0], grad_outbox[0], stash_held[0]
    seq, width = held.shape
    model = width * count
    wq, wkv, wo = w_query[0], w_keyval[0], w_out[0]
    qcols, kvcols = wq.shape[1], wkv.shape[1]
    heads = qcols // HEAD
    shape = jax.ShapeDtypeStruct

    block = sections // 4
    high = sections - block
    near, far = range(block, high), [*range(block), *range(high, sections)]

    def send(value, pairs):
        return lax.ppermute(value, "section", pairs)

    fetched_near = send(stash_held, [(s, sections - 1 - s) for s in near])
    arrived = send(held, [(s, s + 1) for s in range(sections - 1)])
    coming = send(grads_held, [(s + 1, s) for s in range(sections - 1)])
    evicted_near = send(held, [(s, sections - 2 - s) for s in near])
    fetched_far = send(stash_held, [(s, sections - 1 - s) for s in far])
    evicted_far = send(held, [(s, sections - 2 - s) for s in range(block)])
    relayed = send(arrived, [(s, sections - 1 - s) for s in range(high + 1, sections)])
    fetched = jnp.where((position >= block) & (position < high), fetched_near, fetched_far)

    gains = gathered(norm_gain, "tensor")

    x_shard = jnp.where(position == 0, embedded, arrived)
    xs = gathered(x_shard, "tensor")
    normed = pltpu.VMEM((seq, model), BF16)
    shares = [shape((seq, width), BF16)] * count
    proj = 2 * seq * model * (qcols + kvcols)
    out_flops = 2 * seq * model * qcols
    moved = 2 * model * (2 * qcols + kvcols)
    parts = call(
        forward_kernel, count, heads,
        [*xs, *gains, wq, wkv, wo], shares,
        [normed, pltpu.VMEM((seq, qcols), BF16)],
        proj + out_flops, moved,
    )
    mixed = reduced(parts, "tensor")
    section_out = (x_shard.astype(F32) + mixed).astype(BF16)

    bs = gathered(fetched, "tensor")
    query, keyval, prob, inv = call(
        recompute_kernel, count, heads,
        [*bs, *gains, wq, wkv],
        [
            shape((seq, qcols), BF16),
            shape((seq, kvcols), BF16),
            shape((heads, seq, seq), F32),
            shape((seq, HEAD), F32),
        ],
        [normed],
        proj, moved,
    )
    g_shard = jnp.where(position == sections - 1, loss_grad, coming)
    gs = gathered(g_shard, "tensor")
    *terms, total = call(
        backward_kernel, count, heads,
        [*gs, *bs, *gains, query, keyval, prob, wq, wkv, wo],
        [*shares, shape((seq, HEAD), F32)],
        [pltpu.VMEM((seq, qcols), BF16)],
        proj + out_flops, moved,
    )
    place, last, _ = lax.optimization_barrier((position, embedded, total))
    evicted = jnp.where(
        place < block - 1,
        relayed,
        jnp.where(
            place < high - 1, evicted_near, jnp.where(place < sections - 1, evicted_far, last)
        ),
    )
    d_normed = reduced(terms, "tensor")
    total = sum(gathered(total, "tensor"))[:, :1]
    inv = inv[:, :1]
    scaled = d_normed * norm_gain.astype(F32)
    result = (
        g_shard.astype(F32) + inv * scaled - fetched.astype(F32) * inv**3 * (total / model)
    )
    return section_out[None], evicted[None], result.astype(BF16)[None]


def solution(mesh):
    return jax.shard_map(
        local,
        mesh=mesh,
        in_specs=(
            P(None, "tensor"),
            P("section", None, "tensor"),
            P(None, "tensor"),
            P("section", None, "tensor"),
            P("section", None, "tensor"),
            P("section", "tensor"),
            P("section", None, "tensor"),
            P("section", None, "tensor"),
            P("section", "tensor", None),
        ),
        out_specs=(
            P("section", None, "tensor"),
            P("section", None, "tensor"),
            P("section", None, "tensor"),
        ),
        check_vma=False,
    )
```

```python
import functools

import jax
import jax.numpy as jnp
from jax import lax
from jax.experimental import pallas as pl
from jax.experimental.pallas import tpu as pltpu
from jax.sharding import PartitionSpec as P


HEAD = 128
EPS = 1e-05
SCALE = HEAD ** (-0.5)
F32 = jnp.float32
BF16 = jnp.bfloat16

LIMIT = 14 * 2**20


def rotate(value, axis, k):
    count = lax.axis_size(axis)
    return lax.ppermute(value, axis, [(i, (i - k) % count) for i in range(count)])


def gathered(value, axis):
    return [value] + [rotate(value, axis, k) for k in range(1, lax.axis_size(axis))]


def reduced(parts, axis):
    total = parts[0].astype(F32)
    for k in range(1, len(parts)):
        total = total + rotate(parts[k], axis, -k).astype(F32)
    return total


def nt(a, b):
    return lax.dot_general(a, b, (((1,), (1,)), ((), ())), preferred_element_type=F32)


def tn(a, b):
    return lax.dot_general(a, b, (((0,), (0,)), ((), ())), preferred_element_type=F32)


def nn(a, b):
    return jnp.dot(a, b, preferred_element_type=F32)


def vmem_spec():
    return pl.BlockSpec(memory_space=pltpu.VMEM)


def rows_of(ref, col, k, count):
    width = ref.shape[0] // count
    return ref[pl.ds(pl.multiple_of(lax.rem(col + k, count) * width, width), width), :]


def columns_of(ref, col, k, count):
    width = ref.shape[1] // count
    return ref[:, pl.ds(pl.multiple_of(lax.rem(col + k, count) * width, width), width)]


def project(normed, weights, col, count):
    width = weights.shape[0] // count
    total = None
    for k in range(count):
        part = nn(normed[:, k * width : (k + 1) * width], rows_of(weights, col, k, count))
        total = part if total is None else total + part
    return total.astype(BF16)


def normalize(xs, gains, normed):
    width = xs[0].shape[1]
    total = None
    for x in xs:
        xf = x[...].astype(F32)
        part = jnp.sum(xf * xf, axis=-1, keepdims=True)
        total = part if total is None else total + part
    inv = lax.rsqrt(total / (width * len(xs)) + EPS)
    for k, x in enumerate(xs):
        xf = x[...].astype(F32)
        normed[:, k * width : (k + 1) * width] = (xf * inv * gains[k][...].astype(F32)).astype(BF16)
    return inv


def causal_mask(seq):
    rows = lax.broadcasted_iota(jnp.int32, (seq, seq), 0)
    cols = lax.broadcasted_iota(jnp.int32, (seq, seq), 1)
    return rows >= cols


def softmax(query, keys, mask):
    scores = jnp.where(mask, nt(query, keys) * SCALE, -1e30)
    top = jnp.max(scores, axis=-1, keepdims=True)
    weights = jnp.exp(scores - top)
    return weights / jnp.sum(weights, axis=-1, keepdims=True)


def forward_kernel(count, heads, *refs):
    xs, refs = refs[:count], refs[count:]
    gains, refs = refs[:count], refs[count:]
    wq, wkv, wo, refs = *refs[:3], refs[3:]
    outs, (normed, attn) = refs[:count], refs[count:]
    col = lax.axis_index("tensor")
    normalize(xs, gains, normed)
    keyval = project(normed, wkv, col, count)
    query = project(normed, wq, col, count)
    keys, values = keyval[:, :HEAD], keyval[:, HEAD:]
    mask = causal_mask(query.shape[0])
    for h in range(heads):
        prob = softmax(query[:, h * HEAD : (h + 1) * HEAD], keys, mask)
        attn[:, h * HEAD : (h + 1) * HEAD] = nn(prob.astype(BF16), values).astype(BF16)
    for k in reversed(range(count)):
        outs[k][...] = nn(attn[...], columns_of(wo, col, k, count)).astype(BF16)


def recompute_kernel(count, heads, *refs):
    xs, refs = refs[:count], refs[count:]
    gains, refs = refs[:count], refs[count:]
    wq, wkv, query_out, keyval_out, prob_out, inv_out, normed = refs
    col = lax.axis_index("tensor")
    inv = normalize(xs, gains, normed)
    inv_out[...] = jnp.broadcast_to(inv, inv_out.shape)
    keyval = project(normed, wkv, col, count)
    query = project(normed, wq, col, count)
    query_out[...] = query
    keyval_out[...] = keyval
    mask = causal_mask(query.shape[0])
    for h in range(heads):
        prob_out[h] = softmax(query[:, h * HEAD : (h + 1) * HEAD], keyval[:, :HEAD], mask)


def backward_kernel(count, heads, *refs):
    gs, refs = refs[:count], refs[count:]
    xs, refs = refs[:count], refs[count:]
    gains, refs = refs[:count], refs[count:]
    query, keyval, prob, wq, wkv, wo, refs = *refs[:6], refs[6:]
    outs, (total_out, d_query) = refs[:count], refs[count:]
    col = lax.axis_index("tensor")
    d_attn = None
    for k in range(count):
        part = nt(gs[k][...], columns_of(wo, col, k, count))
        d_attn = part if d_attn is None else d_attn + part
    d_attn = d_attn.astype(BF16)
    keys, values = keyval[:, :HEAD], keyval[:, HEAD:]
    d_key = d_value = None
    for h in range(heads):
        span = slice(h * HEAD, (h + 1) * HEAD)
        p = prob[h]
        d_head = d_attn[:, span]
        d_prob = nt(d_head, values)
        d_score = p * (d_prob - jnp.sum(p * d_prob, axis=-1, keepdims=True)) * SCALE
        d_score = d_score.astype(BF16)
        d_query[:, span] = nn(d_score, keys).astype(BF16)
        dk = tn(d_score, query[:, span])
        dv = tn(p.astype(BF16), d_head)
        d_key = dk if d_key is None else d_key + dk
        d_value = dv if d_value is None else d_value + dv
    d_pairs = jnp.concatenate([d_key.astype(BF16), d_value.astype(BF16)], axis=1)
    total = None
    for k in reversed(range(count)):
        term = nt(d_query[...], rows_of(wq, col, k, count))
        term = (term + nt(d_pairs, rows_of(wkv, col, k, count))).astype(BF16)
        outs[k][...] = term
        scaled = term.astype(F32) * gains[k][...].astype(F32)
        part = jnp.sum(scaled * xs[k][...].astype(F32), axis=-1, keepdims=True)
        total = part if total is None else total + part
    total_out[...] = jnp.broadcast_to(total, total_out.shape)


def call(kernel, count, heads, ins, out_shape, scratch, flops, moved):
    return pl.pallas_call(
        functools.partial(kernel, count, heads),
        out_shape=out_shape,
        in_specs=[vmem_spec()] * len(ins),
        out_specs=[vmem_spec()] * len(out_shape),
        scratch_shapes=scratch,
        compiler_params=pltpu.CompilerParams(vmem_limit_bytes=LIMIT),
        cost_estimate=pl.CostEstimate(flops=flops, bytes_accessed=moved, transcendentals=0),
    )(*ins)


def local(
    embedded, outbox, loss_grad, grad_outbox, stash_held, norm_gain, w_query, w_keyval, w_out
):
    sections = lax.axis_size("section")
    count = lax.axis_size("tensor")
    position = lax.axis_index("section")
    held, grads_held, stash_held = outbox[0], grad_outbox[0], stash_held[0]
    seq, width = held.shape
    model = width * count
    wq, wkv, wo = w_query[0], w_keyval[0], w_out[0]
    qcols, kvcols = wq.shape[1], wkv.shape[1]
    heads = qcols // HEAD
    shape = jax.ShapeDtypeStruct

    block = sections // 4
    high = sections - block

    def send(value, pairs):
        return lax.ppermute(value, "section", pairs)

    up = [(s, s + 1) for s in range(sections - 1)]
    crossing = send(held, [(s, t) for s, t in up if t % block == 0])
    fetched = send(stash_held, [(s, sections - 1 - s) for s in range(sections)])
    coming = send(grads_held, [(t, s) for s, t in up])
    inside = send(held, [(s, t) for s, t in up if t % block])
    evicted_near = send(held, [(s, sections - 2 - s) for s in range(block, high)])
    evicted_far = send(held, [(s, sections - 2 - s) for s in range(block)])
    relayed = send(inside, [(s, sections - 1 - s) for s in range(high + 1, sections)])
    gains = gathered(norm_gain, "tensor")

    normed = pltpu.VMEM((seq, model), BF16)
    shares = [shape((seq, width), BF16)] * count
    proj = 2 * seq * model * (qcols + kvcols)
    out_flops = 2 * seq * model * qcols
    moved = 2 * model * (2 * qcols + kvcols)
    bs = gathered(fetched, "tensor")
    query, keyval, prob, inv = call(
        recompute_kernel, count, heads,
        [*bs, *gains, wq, wkv],
        [
            shape((seq, qcols), BF16),
            shape((seq, kvcols), BF16),
            shape((heads, seq, seq), F32),
            shape((seq, HEAD), F32),
        ],
        [normed],
        proj, moved,
    )
    position, _ = lax.optimization_barrier((position, inv))
    arrived = jnp.where(position % block == 0, crossing, inside)
    x_shard = jnp.where(position == 0, embedded, arrived)
    xs = gathered(x_shard, "tensor")
    parts = call(
        forward_kernel, count, heads,
        [*xs, *gains, wq, wkv, wo], shares,
        [normed, pltpu.VMEM((seq, qcols), BF16)],
        proj + out_flops, moved,
    )
    mixed = reduced(parts, "tensor")
    section_out = (x_shard.astype(F32) + mixed).astype(BF16)

    g_shard = jnp.where(position == sections - 1, loss_grad, coming)
    gs = gathered(g_shard, "tensor")
    *terms, total = call(
        backward_kernel, count, heads,
        [*gs, *bs, *gains, query, keyval, prob, wq, wkv, wo],
        [*shares, shape((seq, HEAD), F32)],
        [pltpu.VMEM((seq, qcols), BF16)],
        proj + out_flops, moved,
    )
    d_normed = reduced(terms, "tensor")
    total = sum(gathered(total, "tensor"))[:, :1]
    inv = inv[:, :1]
    scaled = d_normed * norm_gain.astype(F32)
    result = (
        g_shard.astype(F32) + inv * scaled - fetched.astype(F32) * inv**3 * (total / model)
    ).astype(BF16)
    place, last, _ = lax.optimization_barrier((position, embedded, (result, section_out)))
    evicted = jnp.where(
        place < block - 1,
        relayed,
        jnp.where(
            place < high - 1, evicted_near, jnp.where(place < sections - 1, evicted_far, last)
        ),
    )
    return section_out[None], evicted[None], result[None]


def solution(mesh):
    return jax.shard_map(
        local,
        mesh=mesh,
        in_specs=(
            P(None, "tensor"),
            P("section", None, "tensor"),
            P(None, "tensor"),
            P("section", None, "tensor"),
            P("section", None, "tensor"),
            P("section", "tensor"),
            P("section", None, "tensor"),
            P("section", None, "tensor"),
            P("section", "tensor", None),
        ),
        out_specs=(
            P("section", None, "tensor"),
            P("section", None, "tensor"),
            P("section", None, "tensor"),
        ),
        check_vma=False,
    )
```

```python
import functools

import jax
import jax.numpy as jnp
from jax import lax
from jax.experimental import pallas as pl
from jax.experimental.pallas import tpu as pltpu
from jax.sharding import PartitionSpec as P


HEAD = 128
EPS = 1e-05
SCALE = HEAD ** (-0.5)
F32 = jnp.float32
BF16 = jnp.bfloat16

LIMIT = 14 * 2**20


def rotate(value, axis, k):
    count = lax.axis_size(axis)
    return lax.ppermute(value, axis, [(i, (i - k) % count) for i in range(count)])


def gathered(value, axis):
    return [value] + [rotate(value, axis, k) for k in range(1, lax.axis_size(axis))]


def reduced(parts, axis):
    total = parts[0].astype(F32)
    for k in range(1, len(parts)):
        total = total + rotate(parts[k], axis, -k).astype(F32)
    return total


def nt(a, b):
    return lax.dot_general(a, b, (((1,), (1,)), ((), ())), preferred_element_type=F32)


def tn(a, b):
    return lax.dot_general(a, b, (((0,), (0,)), ((), ())), preferred_element_type=F32)


def nn(a, b):
    return jnp.dot(a, b, preferred_element_type=F32)


def vmem_spec():
    return pl.BlockSpec(memory_space=pltpu.VMEM)


def any_spec():
    return pl.BlockSpec(memory_space=pl.ANY)


def rows_of(ref, col, k, count):
    width = ref.shape[0] // count
    return ref[pl.ds(pl.multiple_of(lax.rem(col + k, count) * width, width), width), :]


def columns_of(ref, col, k, count):
    width = ref.shape[1] // count
    return ref[:, pl.ds(pl.multiple_of(lax.rem(col + k, count) * width, width), width)]


def project(normed, weights, col, count):
    width = weights.shape[0] // count
    total = None
    for k in range(count):
        part = nn(normed[:, k * width : (k + 1) * width], rows_of(weights, col, k, count))
        total = part if total is None else total + part
    return total.astype(BF16)


def normalize(xs, gains, normed):
    width = xs[0].shape[1]
    total = None
    for x in xs:
        xf = x[...].astype(F32)
        part = jnp.sum(xf * xf, axis=-1, keepdims=True)
        total = part if total is None else total + part
    inv = lax.rsqrt(total / (width * len(xs)) + EPS)
    for k, x in enumerate(xs):
        xf = x[...].astype(F32)
        normed[:, k * width : (k + 1) * width] = (xf * inv * gains[k][...].astype(F32)).astype(BF16)
    return inv


def causal_mask(seq):
    rows = lax.broadcasted_iota(jnp.int32, (seq, seq), 0)
    cols = lax.broadcasted_iota(jnp.int32, (seq, seq), 1)
    return rows >= cols


def softmax(query, keys, mask):
    scores = jnp.where(mask, nt(query, keys) * SCALE, -1e30)
    top = jnp.max(scores, axis=-1, keepdims=True)
    weights = jnp.exp(scores - top)
    return weights / jnp.sum(weights, axis=-1, keepdims=True)


def forward_kernel(count, heads, *refs):
    xs, refs = refs[:count], refs[count:]
    gains, refs = refs[:count], refs[count:]
    wq, wkv, wo, refs = *refs[:3], refs[3:]
    outs, (normed, attn) = refs[:count], refs[count:]
    col = lax.axis_index("tensor")
    normalize(xs, gains, normed)
    keyval = project(normed, wkv, col, count)
    query = project(normed, wq, col, count)
    keys, values = keyval[:, :HEAD], keyval[:, HEAD:]
    mask = causal_mask(query.shape[0])
    for h in range(heads):
        prob = softmax(query[:, h * HEAD : (h + 1) * HEAD], keys, mask)
        attn[:, h * HEAD : (h + 1) * HEAD] = nn(prob.astype(BF16), values).astype(BF16)
    for k in reversed(range(count)):
        outs[k][...] = nn(attn[...], columns_of(wo, col, k, count)).astype(BF16)


def backward_kernel(count, heads, *refs):
    gs, refs = refs[:count], refs[count:]
    xs, refs = refs[:count], refs[count:]
    gains, refs = refs[:count], refs[count:]
    wq, wkv, wo, refs = *refs[:3], refs[3:]
    outs, (total_out, inv_out, normed, query, prob, d_query) = refs[:count], refs[count:]
    col = lax.axis_index("tensor")
    inv = normalize(xs, gains, normed)
    inv_out[...] = jnp.broadcast_to(inv, inv_out.shape)
    keyval = project(normed, wkv, col, count)
    query[...] = project(normed, wq, col, count)
    mask = causal_mask(query.shape[0])
    for h in range(heads):
        prob[h] = softmax(query[:, h * HEAD : (h + 1) * HEAD], keyval[:, :HEAD], mask)
    d_attn = None
    for k in range(count):
        part = nt(gs[k][...], columns_of(wo, col, k, count))
        d_attn = part if d_attn is None else d_attn + part
    d_attn = d_attn.astype(BF16)
    keys, values = keyval[:, :HEAD], keyval[:, HEAD:]
    d_key = d_value = None
    for h in range(heads):
        span = slice(h * HEAD, (h + 1) * HEAD)
        p = prob[h]
        d_head = d_attn[:, span]
        d_prob = nt(d_head, values)
        d_score = p * (d_prob - jnp.sum(p * d_prob, axis=-1, keepdims=True)) * SCALE
        d_score = d_score.astype(BF16)
        d_query[:, span] = nn(d_score, keys).astype(BF16)
        dk = tn(d_score, query[:, span])
        dv = tn(p.astype(BF16), d_head)
        d_key = dk if d_key is None else d_key + dk
        d_value = dv if d_value is None else d_value + dv
    d_pairs = jnp.concatenate([d_key.astype(BF16), d_value.astype(BF16)], axis=1)
    total = None
    for k in reversed(range(count)):
        term = nt(d_query[...], rows_of(wq, col, k, count))
        term = (term + nt(d_pairs, rows_of(wkv, col, k, count))).astype(BF16)
        outs[k][...] = term
        scaled = term.astype(F32) * gains[k][...].astype(F32)
        part = jnp.sum(scaled * xs[k][...].astype(F32), axis=-1, keepdims=True)
        total = part if total is None else total + part
    total_out[...] = jnp.broadcast_to(total, total_out.shape)


def load_kernel(count, heads, *refs):
    half = (len(refs) - 1) // 2
    sems = refs[-1]
    copies = [
        pltpu.make_async_copy(refs[i], refs[half + i], sems.at[i]) for i in range(half)
    ]
    for copy in copies:
        copy.start()
    for copy in copies:
        copy.wait()


def merge_kernel(count, block, relayed, near, far, last, out, sem):
    place, sections = lax.axis_index("section"), lax.axis_size("section")
    ends = (0, block - 1, sections - block - 1, sections - 1, sections)
    for low, high, source in zip(ends, ends[1:], (relayed, near, far, last)):

        @pl.when((place >= low) & (place < high))
        def _():
            copy = pltpu.make_async_copy(source, out, sem)
            copy.start()
            copy.wait()


def call(kernel, count, heads, ins, out_shape, scratch, flops, moved, far_in=0, far_out=0):
    return pl.pallas_call(
        functools.partial(kernel, count, heads),
        out_shape=out_shape,
        in_specs=[any_spec() if far_in else vmem_spec()] * len(ins),
        out_specs=[any_spec() if far_out else vmem_spec()] * len(out_shape),
        scratch_shapes=scratch,
        compiler_params=pltpu.CompilerParams(vmem_limit_bytes=LIMIT),
        cost_estimate=pl.CostEstimate(flops=flops, bytes_accessed=moved, transcendentals=0),
    )(*ins)


def local(
    embedded, outbox, loss_grad, grad_outbox, stash_held, norm_gain, w_query, w_keyval, w_out
):
    sections = lax.axis_size("section")
    count = lax.axis_size("tensor")
    position = lax.axis_index("section")
    held, grads_held, stash_held = outbox[0], grad_outbox[0], stash_held[0]
    seq, width = held.shape
    model = width * count
    wq, wkv, wo = w_query[0], w_keyval[0], w_out[0]
    qcols, kvcols = wq.shape[1], wkv.shape[1]
    heads = qcols // HEAD
    shape = jax.ShapeDtypeStruct

    block = sections // 4
    high = sections - block

    def send(value, pairs):
        return lax.ppermute(value, "section", pairs)

    up = [(s, s + 1) for s in range(sections - 1)]
    crossing = send(held, [(s, t) for s, t in up if t % block == 0])
    fetched = send(stash_held, [(s, sections - 1 - s) for s in range(sections)])
    coming = send(grads_held, [(t, s) for s, t in up])
    inside = send(held, [(s, t) for s, t in up if t % block])
    evicted_near = send(held, [(s, sections - 2 - s) for s in range(block, high)])
    evicted_far = send(held, [(s, sections - 2 - s) for s in range(block)])
    relayed = send(inside, [(s, sections - 1 - s) for s in range(high + 1, sections)])
    gains = gathered(norm_gain, "tensor")

    normed = pltpu.VMEM((seq, model), BF16)
    shares = [shape((seq, width), BF16)] * count
    proj = 2 * seq * model * (qcols + kvcols)
    out_flops = 2 * seq * model * qcols
    moved = 2 * model * (2 * qcols + kvcols)
    wq, wkv, wo = call(
        load_kernel, count, heads, [wq, wkv, wo],
        [shape(w.shape, w.dtype) for w in (wq, wkv, wo)],
        [pltpu.SemaphoreType.DMA((3,))], 0, 2 * moved, far_in=1,
    )
    bs = gathered(fetched, "tensor")
    arrived = jnp.where(position % block == 0, crossing, inside)
    x_shard = jnp.where(position == 0, embedded, arrived)
    xs = gathered(x_shard, "tensor")
    parts = call(
        forward_kernel, count, heads,
        [*xs, *gains, wq, wkv, wo], shares,
        [normed, pltpu.VMEM((seq, qcols), BF16)],
        proj + out_flops, moved,
    )
    mixed = reduced(parts, "tensor")
    section_out = (x_shard.astype(F32) + mixed).astype(BF16)

    g_shard = jnp.where(position == sections - 1, loss_grad, coming)
    gs = gathered(g_shard, "tensor")
    *terms, total, inv = call(
        backward_kernel, count, heads,
        [*gs, *bs, *gains, wq, wkv, wo],
        [*shares, shape((seq, HEAD), F32), shape((seq, HEAD), F32)],
        [
            normed,
            pltpu.VMEM((seq, qcols), BF16),
            pltpu.VMEM((heads, seq, seq), F32),
            pltpu.VMEM((seq, qcols), BF16),
        ],
        2 * proj + out_flops, moved,
    )
    d_normed = reduced(terms, "tensor")
    total = sum(gathered(total, "tensor"))[:, :1]
    inv = inv[:, :1]
    scaled = d_normed * norm_gain.astype(F32)
    result = (
        g_shard.astype(F32) + inv * scaled - fetched.astype(F32) * inv**3 * (total / model)
    ).astype(BF16)
    last, _ = lax.optimization_barrier((embedded, (result, section_out)))
    (evicted,) = call(
        merge_kernel, count, block,
        [relayed, evicted_near, evicted_far, last], [shape((seq, width), BF16)],
        [pltpu.SemaphoreType.DMA], 0, 4 * seq * width, far_out=1,
    )
    return section_out[None], evicted[None], result[None]


def solution(mesh):
    return jax.shard_map(
        local,
        mesh=mesh,
        in_specs=(
            P(None, "tensor"),
            P("section", None, "tensor"),
            P(None, "tensor"),
            P("section", None, "tensor"),
            P("section", None, "tensor"),
            P("section", "tensor"),
            P("section", None, "tensor"),
            P("section", None, "tensor"),
            P("section", "tensor", None),
        ),
        out_specs=(
            P("section", None, "tensor"),
            P("section", None, "tensor"),
            P("section", None, "tensor"),
        ),
        check_vma=False,
    )
```

```python
import functools

import jax
import jax.numpy as jnp
from jax import lax
from jax.experimental import pallas as pl
from jax.experimental.pallas import tpu as pltpu
from jax.sharding import PartitionSpec as P


HEAD = 128
EPS = 1e-05
SCALE = HEAD ** (-0.5)
F32 = jnp.float32
BF16 = jnp.bfloat16

LIMIT = 14 * 2**20


def rotate(value, axis, k):
    count = lax.axis_size(axis)
    return lax.ppermute(value, axis, [(i, (i - k) % count) for i in range(count)])


def gathered(value, axis):
    return [value] + [rotate(value, axis, k) for k in range(1, lax.axis_size(axis))]


def reduced(parts, axis):
    total = parts[0].astype(F32)
    for k in range(1, len(parts)):
        total = total + rotate(parts[k], axis, -k).astype(F32)
    return total


def nt(a, b):
    return lax.dot_general(a, b, (((1,), (1,)), ((), ())), preferred_element_type=F32)


def tn(a, b):
    return lax.dot_general(a, b, (((0,), (0,)), ((), ())), preferred_element_type=F32)


def nn(a, b):
    return jnp.dot(a, b, preferred_element_type=F32)


def vmem_spec():
    return pl.BlockSpec(memory_space=pltpu.VMEM)


def any_spec():
    return pl.BlockSpec(memory_space=pl.ANY)


def rows_of(ref, col, k, count):
    width = ref.shape[0] // count
    return ref[pl.ds(pl.multiple_of(lax.rem(col + k, count) * width, width), width), :]


def columns_of(ref, col, k, count):
    width = ref.shape[1] // count
    return ref[:, pl.ds(pl.multiple_of(lax.rem(col + k, count) * width, width), width)]


def project(normed, weights, col, count):
    width = weights.shape[0] // count
    total = None
    for k in range(count):
        part = nn(normed[:, k * width : (k + 1) * width], rows_of(weights, col, k, count))
        total = part if total is None else total + part
    return total.astype(BF16)


def normalize(xs, gains, normed):
    width = xs[0].shape[1]
    total = None
    for x in xs:
        xf = x[...].astype(F32)
        part = jnp.sum(xf * xf, axis=-1, keepdims=True)
        total = part if total is None else total + part
    inv = lax.rsqrt(total / (width * len(xs)) + EPS)
    for k, x in enumerate(xs):
        xf = x[...].astype(F32)
        normed[:, k * width : (k + 1) * width] = (xf * inv * gains[k][...].astype(F32)).astype(BF16)
    return inv


def causal_mask(seq):
    rows = lax.broadcasted_iota(jnp.int32, (seq, seq), 0)
    cols = lax.broadcasted_iota(jnp.int32, (seq, seq), 1)
    return rows >= cols


def softmax(query, keys, mask):
    scores = jnp.where(mask, nt(query, keys) * SCALE, -1e30)
    top = jnp.max(scores, axis=-1, keepdims=True)
    weights = jnp.exp(scores - top)
    return weights / jnp.sum(weights, axis=-1, keepdims=True)


def forward_kernel(count, heads, *refs):
    xs, refs = refs[:count], refs[count:]
    gains, refs = refs[:count], refs[count:]
    wq, wkv, wo, refs = *refs[:3], refs[3:]
    outs, (normed, attn) = refs[:count], refs[count:]
    col = lax.axis_index("tensor")
    normalize(xs, gains, normed)
    keyval = project(normed, wkv, col, count)
    query = project(normed, wq, col, count)
    keys, values = keyval[:, :HEAD], keyval[:, HEAD:]
    mask = causal_mask(query.shape[0])
    for h in range(heads):
        prob = softmax(query[:, h * HEAD : (h + 1) * HEAD], keys, mask)
        attn[:, h * HEAD : (h + 1) * HEAD] = nn(prob.astype(BF16), values).astype(BF16)
    for k in reversed(range(count)):
        outs[k][...] = nn(attn[...], columns_of(wo, col, k, count)).astype(BF16)


def backward_kernel(count, heads, *refs):
    gs, refs = refs[:count], refs[count:]
    xs, refs = refs[:count], refs[count:]
    gains, refs = refs[:count], refs[count:]
    wq, wkv, wo, refs = *refs[:3], refs[3:]
    outs, (total_out, inv_out, normed, query, prob, d_query) = refs[:count], refs[count:]
    col = lax.axis_index("tensor")
    inv = normalize(xs, gains, normed)
    inv_out[...] = jnp.broadcast_to(inv, inv_out.shape)
    keyval = project(normed, wkv, col, count)
    query[...] = project(normed, wq, col, count)
    mask = causal_mask(query.shape[0])
    for h in range(heads):
        prob[h] = softmax(query[:, h * HEAD : (h + 1) * HEAD], keyval[:, :HEAD], mask)
    d_attn = None
    for k in range(count):
        part = nt(gs[k][...], columns_of(wo, col, k, count))
        d_attn = part if d_attn is None else d_attn + part
    d_attn = d_attn.astype(BF16)
    keys, values = keyval[:, :HEAD], keyval[:, HEAD:]
    d_key = d_value = None
    for h in range(heads):
        span = slice(h * HEAD, (h + 1) * HEAD)
        p = prob[h]
        d_head = d_attn[:, span]
        d_prob = nt(d_head, values)
        d_score = p * (d_prob - jnp.sum(p * d_prob, axis=-1, keepdims=True)) * SCALE
        d_score = d_score.astype(BF16)
        d_query[:, span] = nn(d_score, keys).astype(BF16)
        dk = tn(d_score, query[:, span])
        dv = tn(p.astype(BF16), d_head)
        d_key = dk if d_key is None else d_key + dk
        d_value = dv if d_value is None else d_value + dv
    d_pairs = jnp.concatenate([d_key.astype(BF16), d_value.astype(BF16)], axis=1)
    total = None
    for k in reversed(range(count)):
        term = nt(d_query[...], rows_of(wq, col, k, count))
        term = (term + nt(d_pairs, rows_of(wkv, col, k, count))).astype(BF16)
        outs[k][...] = term
        scaled = term.astype(F32) * gains[k][...].astype(F32)
        part = jnp.sum(scaled * xs[k][...].astype(F32), axis=-1, keepdims=True)
        total = part if total is None else total + part
    total_out[...] = jnp.broadcast_to(total, total_out.shape)


def load_kernel(count, heads, *refs):
    half = (len(refs) - 1) // 2
    sems = refs[-1]
    copies = [
        pltpu.make_async_copy(refs[i], refs[half + i], sems.at[i]) for i in range(half)
    ]
    for copy in copies:
        copy.start()
    for copy in copies:
        copy.wait()


def choose_kernel(count, tests, *refs):
    *sources, out, sem = refs
    place, sections = lax.axis_index("section"), lax.axis_size("section")
    for test, source in zip(tests(place, sections), sources):

        @pl.when(test)
        def _():
            copy = pltpu.make_async_copy(source, out, sem)
            copy.start()
            copy.wait()


def merge_kernel(count, block, relayed, alone, direct, last, out, sem):
    place, sections = lax.axis_index("section"), lax.axis_size("section")
    is_last = place == sections - 1
    is_alone = place == sections - 1 - block
    is_relayed = place < block - 1
    is_direct = jnp.logical_not(is_last | is_alone | is_relayed)
    chosen = ((is_relayed, relayed), (is_alone, alone), (is_direct, direct), (is_last, last))
    for here, source in chosen:

        @pl.when(here)
        def _():
            copy = pltpu.make_async_copy(source, out, sem)
            copy.start()
            copy.wait()


def call(kernel, count, heads, ins, out_shape, scratch, flops, moved, far_in=0, far_out=0):
    return pl.pallas_call(
        functools.partial(kernel, count, heads),
        out_shape=out_shape,
        in_specs=[any_spec() if far_in else vmem_spec()] * len(ins),
        out_specs=[any_spec() if far_out else vmem_spec()] * len(out_shape),
        scratch_shapes=scratch,
        compiler_params=pltpu.CompilerParams(vmem_limit_bytes=LIMIT),
        cost_estimate=pl.CostEstimate(flops=flops, bytes_accessed=moved, transcendentals=0),
    )(*ins)


def local(
    embedded, outbox, loss_grad, grad_outbox, stash_held, norm_gain, w_query, w_keyval, w_out
):
    sections = lax.axis_size("section")
    count = lax.axis_size("tensor")
    held, grads_held, stash_held = outbox[0], grad_outbox[0], stash_held[0]
    seq, width = held.shape
    model = width * count
    wq, wkv, wo = w_query[0], w_keyval[0], w_out[0]
    qcols, kvcols = wq.shape[1], wkv.shape[1]
    heads = qcols // HEAD
    shape = jax.ShapeDtypeStruct

    block = sections // 4
    high = sections - block

    def send(value, pairs):
        return lax.ppermute(value, "section", pairs)

    def early(t):
        return (t % block == 0) | (t > high)

    up = [(s, s + 1) for s in range(sections - 1)]
    soon = send(held, [(s, t) for s, t in up if early(t)])
    coming = send(grads_held, [(t, s) for s, t in up])
    fetched = send(stash_held, [(s, sections - 1 - s) for s in range(sections)])
    later = send(held, [(s, t) for s, t in up if not early(t)])
    evicted = send(held, [(s, sections - 2 - s) for s in range(high) if s != block - 1])
    alone = send(held, [(block - 1, sections - 1 - block)])
    relayed = send(soon, [(s, sections - 1 - s) for s in range(high + 1, sections)])
    gains = gathered(norm_gain, "tensor")

    normed = pltpu.VMEM((seq, model), BF16)
    shares = [shape((seq, width), BF16)] * count
    proj = 2 * seq * model * (qcols + kvcols)
    out_flops = 2 * seq * model * qcols
    moved = 2 * model * (2 * qcols + kvcols)
    wq, wkv, wo = call(
        load_kernel, count, heads, [wq, wkv, wo],
        [shape(w.shape, w.dtype) for w in (wq, wkv, wo)],
        [pltpu.SemaphoreType.DMA((3,))], 0, 2 * moved, far_in=1,
    )
    bs = gathered(fetched, "tensor")

    def x_tests(place, sections):
        is_early = (place % block == 0) | (place > high)
        return place == 0, is_early & (place != 0), jnp.logical_not(is_early)

    def choose(tests, ins):
        (out,) = call(
            choose_kernel, count, tests, ins, [shape((seq, width), BF16)],
            [pltpu.SemaphoreType.DMA], 0, 4 * seq * width,
        )
        return out

    x_shard = choose(x_tests, [embedded, soon, later])
    xs = gathered(x_shard, "tensor")
    parts = call(
        forward_kernel, count, heads,
        [*xs, *gains, wq, wkv, wo], shares,
        [normed, pltpu.VMEM((seq, qcols), BF16)],
        proj + out_flops, moved,
    )
    g_shard = choose(lambda place, n: (place == n - 1, place != n - 1), [loss_grad, coming])
    gs = gathered(g_shard, "tensor")
    *terms, total, inv = call(
        backward_kernel, count, heads,
        [*gs, *bs, *gains, wq, wkv, wo],
        [*shares, shape((seq, HEAD), F32), shape((seq, HEAD), F32)],
        [
            normed,
            pltpu.VMEM((seq, qcols), BF16),
            pltpu.VMEM((heads, seq, seq), F32),
            pltpu.VMEM((seq, qcols), BF16),
        ],
        2 * proj + out_flops, moved,
    )
    d_normed = reduced(terms, "tensor")
    total = sum(gathered(total, "tensor"))[:, :1]
    inv = inv[:, :1]
    scaled = d_normed * norm_gain.astype(F32)
    result = (
        g_shard.astype(F32) + inv * scaled - fetched.astype(F32) * inv**3 * (total / model)
    ).astype(BF16)
    own, *others = parts
    own, _ = lax.optimization_barrier((own, result))
    mixed = reduced([own, *others], "tensor")
    section_out = (x_shard.astype(F32) + mixed).astype(BF16)
    last, _ = lax.optimization_barrier((embedded, (result, section_out)))
    (evicted,) = call(
        merge_kernel, count, block,
        [relayed, alone, evicted, last], [shape((seq, width), BF16)],
        [pltpu.SemaphoreType.DMA], 0, 4 * seq * width, far_out=1,
    )
    return section_out[None], evicted[None], result[None]


def solution(mesh):
    return jax.shard_map(
        local,
        mesh=mesh,
        in_specs=(
            P(None, "tensor"),
            P("section", None, "tensor"),
            P(None, "tensor"),
            P("section", None, "tensor"),
            P("section", None, "tensor"),
            P("section", "tensor"),
            P("section", None, "tensor"),
            P("section", None, "tensor"),
            P("section", "tensor", None),
        ),
        out_specs=(
            P("section", None, "tensor"),
            P("section", None, "tensor"),
            P("section", None, "tensor"),
        ),
        check_vma=False,
    )
```

```python
import functools

import jax
import jax.numpy as jnp
from jax import lax
from jax.experimental import pallas as pl
from jax.experimental.pallas import tpu as pltpu
from jax.sharding import PartitionSpec as P


HEAD = 128
EPS = 1e-05
SCALE = HEAD ** (-0.5)
F32 = jnp.float32
BF16 = jnp.bfloat16

LIMIT = 14 * 2**20


def rotate(value, axis, k):
    count = lax.axis_size(axis)
    return lax.ppermute(value, axis, [(i, (i - k) % count) for i in range(count)])


def gathered(value, axis):
    return [value] + [rotate(value, axis, k) for k in range(1, lax.axis_size(axis))]


def reduced(parts, axis):
    total = parts[0].astype(F32)
    for k in range(1, len(parts)):
        total = total + rotate(parts[k], axis, -k).astype(F32)
    return total


def nt(a, b):
    return lax.dot_general(a, b, (((1,), (1,)), ((), ())), preferred_element_type=F32)


def tn(a, b):
    return lax.dot_general(a, b, (((0,), (0,)), ((), ())), preferred_element_type=F32)


def nn(a, b):
    return jnp.dot(a, b, preferred_element_type=F32)


def vmem_spec():
    return pl.BlockSpec(memory_space=pltpu.VMEM)


def any_spec():
    return pl.BlockSpec(memory_space=pl.ANY)


def rows_of(ref, col, k, count):
    width = ref.shape[0] // count
    return ref[pl.ds(pl.multiple_of(lax.rem(col + k, count) * width, width), width), :]


def columns_of(ref, col, k, count):
    width = ref.shape[1] // count
    return ref[:, pl.ds(pl.multiple_of(lax.rem(col + k, count) * width, width), width)]


def project(normed, weights, col, count):
    width = weights.shape[0] // count
    total = None
    for k in range(count):
        part = nn(normed[:, k * width : (k + 1) * width], rows_of(weights, col, k, count))
        total = part if total is None else total + part
    return total.astype(BF16)


def normalize(xs, gains, normed):
    width = xs[0].shape[1]
    total = None
    for x in xs:
        xf = x[...].astype(F32)
        part = jnp.sum(xf * xf, axis=-1, keepdims=True)
        total = part if total is None else total + part
    inv = lax.rsqrt(total / (width * len(xs)) + EPS)
    for k, x in enumerate(xs):
        xf = x[...].astype(F32)
        normed[:, k * width : (k + 1) * width] = (xf * inv * gains[k][...].astype(F32)).astype(BF16)
    return inv


def causal_mask(seq):
    rows = lax.broadcasted_iota(jnp.int32, (seq, seq), 0)
    cols = lax.broadcasted_iota(jnp.int32, (seq, seq), 1)
    return rows >= cols


def softmax(query, keys, mask):
    scores = jnp.where(mask, nt(query, keys) * SCALE, -1e30)
    top = jnp.max(scores, axis=-1, keepdims=True)
    weights = jnp.exp(scores - top)
    return weights / jnp.sum(weights, axis=-1, keepdims=True)


def forward_kernel(count, heads, *refs):
    xs, refs = refs[:count], refs[count:]
    gains, refs = refs[:count], refs[count:]
    wq, wkv, wo, refs = *refs[:3], refs[3:]
    outs, (normed, attn) = refs[:count], refs[count:]
    col = lax.axis_index("tensor")
    normalize(xs, gains, normed)
    keyval = project(normed, wkv, col, count)
    query = project(normed, wq, col, count)
    keys, values = keyval[:, :HEAD], keyval[:, HEAD:]
    mask = causal_mask(query.shape[0])
    for h in range(heads):
        prob = softmax(query[:, h * HEAD : (h + 1) * HEAD], keys, mask)
        attn[:, h * HEAD : (h + 1) * HEAD] = nn(prob.astype(BF16), values).astype(BF16)
    for k in reversed(range(count)):
        outs[k][...] = nn(attn[...], columns_of(wo, col, k, count)).astype(BF16)


def backward_kernel(count, heads, *refs):
    gs, refs = refs[:count], refs[count:]
    xs, refs = refs[:count], refs[count:]
    gains, refs = refs[:count], refs[count:]
    wq, wkv, wo, refs = *refs[:3], refs[3:]
    outs, (total_out, inv_out, normed, query, prob, d_query) = refs[:count], refs[count:]
    col = lax.axis_index("tensor")
    inv = normalize(xs, gains, normed)
    inv_out[...] = jnp.broadcast_to(inv, inv_out.shape)
    keyval = project(normed, wkv, col, count)
    query[...] = project(normed, wq, col, count)
    mask = causal_mask(query.shape[0])
    for h in range(heads):
        prob[h] = softmax(query[:, h * HEAD : (h + 1) * HEAD], keyval[:, :HEAD], mask)
    d_attn = None
    for k in range(count):
        part = nt(gs[k][...], columns_of(wo, col, k, count))
        d_attn = part if d_attn is None else d_attn + part
    d_attn = d_attn.astype(BF16)
    keys, values = keyval[:, :HEAD], keyval[:, HEAD:]
    d_key = d_value = None
    for h in range(heads):
        span = slice(h * HEAD, (h + 1) * HEAD)
        p = prob[h]
        d_head = d_attn[:, span]
        d_prob = nt(d_head, values)
        d_score = p * (d_prob - jnp.sum(p * d_prob, axis=-1, keepdims=True)) * SCALE
        d_score = d_score.astype(BF16)
        d_query[:, span] = nn(d_score, keys).astype(BF16)
        dk = tn(d_score, query[:, span])
        dv = tn(p.astype(BF16), d_head)
        d_key = dk if d_key is None else d_key + dk
        d_value = dv if d_value is None else d_value + dv
    d_pairs = jnp.concatenate([d_key.astype(BF16), d_value.astype(BF16)], axis=1)
    total = None
    for k in reversed(range(count)):
        term = nt(d_query[...], rows_of(wq, col, k, count))
        term = (term + nt(d_pairs, rows_of(wkv, col, k, count))).astype(BF16)
        outs[k][...] = term
        scaled = term.astype(F32) * gains[k][...].astype(F32)
        part = jnp.sum(scaled * xs[k][...].astype(F32), axis=-1, keepdims=True)
        total = part if total is None else total + part
    total_out[...] = jnp.broadcast_to(total, total_out.shape)


def load_kernel(count, heads, *refs):
    half = (len(refs) - 1) // 2
    sems = refs[-1]
    copies = [
        pltpu.make_async_copy(refs[i], refs[half + i], sems.at[i]) for i in range(half)
    ]
    for copy in copies:
        copy.start()
    for copy in copies:
        copy.wait()


def choose_kernel(count, tests, *refs):
    *sources, out, sem = refs
    place, sections = lax.axis_index("section"), lax.axis_size("section")
    for test, source in zip(tests(place, sections), sources):

        @pl.when(test)
        def _():
            copy = pltpu.make_async_copy(source, out, sem)
            copy.start()
            copy.wait()


def merge_kernel(count, block, relayed, alone, direct, last, out, sem):
    place, sections = lax.axis_index("section"), lax.axis_size("section")
    is_last = place == sections - 1
    is_alone = place == sections - 1 - block
    is_relayed = place < block - 1
    is_direct = jnp.logical_not(is_last | is_alone | is_relayed)
    chosen = ((is_relayed, relayed), (is_alone, alone), (is_direct, direct), (is_last, last))
    for here, source in chosen:

        @pl.when(here)
        def _():
            copy = pltpu.make_async_copy(source, out, sem)
            copy.start()
            copy.wait()


def call(kernel, count, heads, ins, out_shape, scratch, flops, moved, far_in=0, far_out=0):
    return pl.pallas_call(
        functools.partial(kernel, count, heads),
        out_shape=out_shape,
        in_specs=[any_spec() if far_in else vmem_spec()] * len(ins),
        out_specs=[any_spec() if far_out else vmem_spec()] * len(out_shape),
        scratch_shapes=scratch,
        compiler_params=pltpu.CompilerParams(vmem_limit_bytes=LIMIT),
        cost_estimate=pl.CostEstimate(flops=flops, bytes_accessed=moved, transcendentals=0),
    )(*ins)


def local(
    embedded, outbox, loss_grad, grad_outbox, stash_held, norm_gain, w_query, w_keyval, w_out
):
    sections = lax.axis_size("section")
    count = lax.axis_size("tensor")
    held, grads_held, stash_held = outbox[0], grad_outbox[0], stash_held[0]
    seq, width = held.shape
    model = width * count
    wq, wkv, wo = w_query[0], w_keyval[0], w_out[0]
    qcols, kvcols = wq.shape[1], wkv.shape[1]
    heads = qcols // HEAD
    shape = jax.ShapeDtypeStruct

    block = sections // 4
    high = sections - block

    def send(value, pairs):
        return lax.ppermute(value, "section", pairs)

    def early(t):
        return (t % block == 0) | (t > high)

    up = [(s, s + 1) for s in range(sections - 1)]
    soon = send(held, [(s, t) for s, t in up if early(t)])
    coming = send(grads_held, [(t, s) for s, t in up])
    fetched = send(stash_held, [(s, sections - 1 - s) for s in range(sections)])
    later = send(held, [(s, t) for s, t in up if not early(t)])
    evicted = send(held, [(s, sections - 2 - s) for s in range(high) if s != block - 1])
    alone = send(held, [(block - 1, sections - 1 - block)])
    relayed = send(soon, [(s, sections - 1 - s) for s in range(high + 1, sections)])
    gains = gathered(norm_gain, "tensor")

    normed = pltpu.VMEM((seq, model), BF16)
    shares = [shape((seq, width), BF16)] * count
    proj = 2 * seq * model * (qcols + kvcols)
    out_flops = 2 * seq * model * qcols
    moved = 2 * model * (2 * qcols + kvcols)
    wq, wkv, wo = call(
        load_kernel, count, heads, [wq, wkv, wo],
        [shape(w.shape, w.dtype) for w in (wq, wkv, wo)],
        [pltpu.SemaphoreType.DMA((3,))], 0, 2 * moved, far_in=1,
    )
    bs = gathered(fetched, "tensor")

    def x_tests(place, sections):
        is_early = (place % block == 0) | (place > high)
        return place == 0, is_early & (place != 0), jnp.logical_not(is_early)

    def choose(tests, ins):
        (out,) = call(
            choose_kernel, count, tests, ins, [shape((seq, width), BF16)],
            [pltpu.SemaphoreType.DMA], 0, 4 * seq * width,
        )
        return out

    x_shard = choose(x_tests, [embedded, soon, later])
    xs = gathered(x_shard, "tensor")
    parts = call(
        forward_kernel, count, heads,
        [*xs, *gains, wq, wkv, wo], shares,
        [normed, pltpu.VMEM((seq, qcols), BF16)],
        proj + out_flops, moved,
    )
    g_shard = choose(lambda place, n: (place == n - 1, place != n - 1), [loss_grad, coming])
    gs = gathered(g_shard, "tensor")
    *terms, total, inv = call(
        backward_kernel, count, heads,
        [*gs, *bs, *gains, wq, wkv, wo],
        [*shares, shape((seq, HEAD), F32), shape((seq, HEAD), F32)],
        [
            normed,
            pltpu.VMEM((seq, qcols), BF16),
            pltpu.VMEM((heads, seq, seq), F32),
            pltpu.VMEM((seq, qcols), BF16),
        ],
        2 * proj + out_flops, moved,
    )
    mixed = reduced(parts, "tensor")
    section_out = (x_shard.astype(F32) + mixed).astype(BF16)
    own, *others = terms
    own, _ = lax.optimization_barrier((own, section_out))
    d_normed = reduced([own, *others], "tensor")
    total = sum(gathered(total, "tensor"))[:, :1]
    inv = inv[:, :1]
    scaled = d_normed * norm_gain.astype(F32)
    result = (
        g_shard.astype(F32) + inv * scaled - fetched.astype(F32) * inv**3 * (total / model)
    ).astype(BF16)
    last, _ = lax.optimization_barrier((embedded, (result, section_out)))
    (evicted,) = call(
        merge_kernel, count, block,
        [relayed, alone, evicted, last], [shape((seq, width), BF16)],
        [pltpu.SemaphoreType.DMA], 0, 4 * seq * width, far_out=1,
    )
    return section_out[None], evicted[None], result[None]


def solution(mesh):
    return jax.shard_map(
        local,
        mesh=mesh,
        in_specs=(
            P(None, "tensor"),
            P("section", None, "tensor"),
            P(None, "tensor"),
            P("section", None, "tensor"),
            P("section", None, "tensor"),
            P("section", "tensor"),
            P("section", None, "tensor"),
            P("section", None, "tensor"),
            P("section", "tensor", None),
        ),
        out_specs=(
            P("section", None, "tensor"),
            P("section", None, "tensor"),
            P("section", None, "tensor"),
        ),
        check_vma=False,
    )
```

```python
import functools

import jax
import jax.numpy as jnp
from jax import lax
from jax.experimental import pallas as pl
from jax.experimental.pallas import tpu as pltpu
from jax.sharding import PartitionSpec as P


HEAD = 128
EPS = 1e-05
SCALE = HEAD ** (-0.5)
F32 = jnp.float32
BF16 = jnp.bfloat16

LIMIT = 14 * 2**20


def rotate(value, axis, k):
    count = lax.axis_size(axis)
    return lax.ppermute(value, axis, [(i, (i - k) % count) for i in range(count)])


def gathered(value, axis):
    return [value] + [rotate(value, axis, k) for k in range(1, lax.axis_size(axis))]


def reduced(parts, axis):
    total = parts[0].astype(F32)
    for k in range(1, len(parts)):
        total = total + rotate(parts[k], axis, -k).astype(F32)
    return total


def nt(a, b):
    return lax.dot_general(a, b, (((1,), (1,)), ((), ())), preferred_element_type=F32)


def tn(a, b):
    return lax.dot_general(a, b, (((0,), (0,)), ((), ())), preferred_element_type=F32)


def nn(a, b):
    return jnp.dot(a, b, preferred_element_type=F32)


def vmem_spec():
    return pl.BlockSpec(memory_space=pltpu.VMEM)


def any_spec():
    return pl.BlockSpec(memory_space=pl.ANY)


def rows_of(ref, col, k, count):
    width = ref.shape[0] // count
    return ref[pl.ds(pl.multiple_of(lax.rem(col + k, count) * width, width), width), :]


def columns_of(ref, col, k, count):
    width = ref.shape[1] // count
    return ref[:, pl.ds(pl.multiple_of(lax.rem(col + k, count) * width, width), width)]


def project(normed, weights, col, count):
    width = weights.shape[0] // count
    total = None
    for k in range(count):
        part = nn(normed[:, k * width : (k + 1) * width], rows_of(weights, col, k, count))
        total = part if total is None else total + part
    return total.astype(BF16)


def normalize(xs, gains, normed):
    width = xs[0].shape[1]
    total = None
    for x in xs:
        xf = x[...].astype(F32)
        part = jnp.sum(xf * xf, axis=-1, keepdims=True)
        total = part if total is None else total + part
    inv = lax.rsqrt(total / (width * len(xs)) + EPS)
    for k, x in enumerate(xs):
        xf = x[...].astype(F32)
        normed[:, k * width : (k + 1) * width] = (xf * inv * gains[k][...].astype(F32)).astype(BF16)
    return inv


def causal_mask(seq):
    rows = lax.broadcasted_iota(jnp.int32, (seq, seq), 0)
    cols = lax.broadcasted_iota(jnp.int32, (seq, seq), 1)
    return rows >= cols


def softmax(query, keys, mask):
    scores = jnp.where(mask, nt(query, keys) * SCALE, -1e30)
    top = jnp.max(scores, axis=-1, keepdims=True)
    weights = jnp.exp(scores - top)
    return weights / jnp.sum(weights, axis=-1, keepdims=True)


def forward_kernel(count, heads, *refs):
    xs, refs = refs[:count], refs[count:]
    gains, refs = refs[:count], refs[count:]
    wq, wkv, wo, refs = *refs[:3], refs[3:]
    outs, (normed, attn) = refs[:count], refs[count:]
    col = lax.axis_index("tensor")
    normalize(xs, gains, normed)
    keyval = project(normed, wkv, col, count)
    query = project(normed, wq, col, count)
    keys, values = keyval[:, :HEAD], keyval[:, HEAD:]
    mask = causal_mask(query.shape[0])
    for h in range(heads):
        prob = softmax(query[:, h * HEAD : (h + 1) * HEAD], keys, mask)
        attn[:, h * HEAD : (h + 1) * HEAD] = nn(prob.astype(BF16), values).astype(BF16)
    for k in reversed(range(count)):
        outs[k][...] = nn(attn[...], columns_of(wo, col, k, count)).astype(BF16)


def backward_kernel(count, heads, *refs):
    gs, refs = refs[:count], refs[count:]
    xs, refs = refs[:count], refs[count:]
    gains, refs = refs[:count], refs[count:]
    wq, wkv, wo, refs = *refs[:3], refs[3:]
    outs, (total_out, inv_out, normed, query, prob, d_query) = refs[:count], refs[count:]
    col = lax.axis_index("tensor")
    inv = normalize(xs, gains, normed)
    inv_out[...] = jnp.broadcast_to(inv, inv_out.shape)
    keyval = project(normed, wkv, col, count)
    query[...] = project(normed, wq, col, count)
    mask = causal_mask(query.shape[0])
    for h in range(heads):
        prob[h] = softmax(query[:, h * HEAD : (h + 1) * HEAD], keyval[:, :HEAD], mask)
    d_attn = None
    for k in range(count):
        part = nt(gs[k][...], columns_of(wo, col, k, count))
        d_attn = part if d_attn is None else d_attn + part
    d_attn = d_attn.astype(BF16)
    keys, values = keyval[:, :HEAD], keyval[:, HEAD:]
    d_key = d_value = None
    for h in range(heads):
        span = slice(h * HEAD, (h + 1) * HEAD)
        p = prob[h]
        d_head = d_attn[:, span]
        d_prob = nt(d_head, values)
        d_score = p * (d_prob - jnp.sum(p * d_prob, axis=-1, keepdims=True)) * SCALE
        d_score = d_score.astype(BF16)
        d_query[:, span] = nn(d_score, keys).astype(BF16)
        dk = tn(d_score, query[:, span])
        dv = tn(p.astype(BF16), d_head)
        d_key = dk if d_key is None else d_key + dk
        d_value = dv if d_value is None else d_value + dv
    d_pairs = jnp.concatenate([d_key.astype(BF16), d_value.astype(BF16)], axis=1)
    total = None
    for k in reversed(range(count)):
        term = nt(d_query[...], rows_of(wq, col, k, count))
        term = (term + nt(d_pairs, rows_of(wkv, col, k, count))).astype(BF16)
        outs[k][...] = term
        scaled = term.astype(F32) * gains[k][...].astype(F32)
        part = jnp.sum(scaled * xs[k][...].astype(F32), axis=-1, keepdims=True)
        total = part if total is None else total + part
    total_out[...] = jnp.broadcast_to(total, total_out.shape)


def load_kernel(count, heads, *refs):
    half = (len(refs) - 1) // 2
    sems = refs[-1]
    copies = [
        pltpu.make_async_copy(refs[i], refs[half + i], sems.at[i]) for i in range(half)
    ]
    for copy in copies:
        copy.start()
    for copy in copies:
        copy.wait()


def choose_kernel(count, tests, *refs):
    *sources, out, sem = refs
    place, sections = lax.axis_index("section"), lax.axis_size("section")
    for test, source in zip(tests(place, sections), sources):

        @pl.when(test)
        def _():
            copy = pltpu.make_async_copy(source, out, sem)
            copy.start()
            copy.wait()


def merge_kernel(count, block, relayed, rest, alone, direct, last, out, sem):
    place, sections = lax.axis_index("section"), lax.axis_size("section")
    is_last = place == sections - 1
    is_alone = place == sections - 1 - block
    is_relayed = place < block - 1
    is_direct = jnp.logical_not(is_last | is_alone | is_relayed)

    @pl.when(is_relayed)
    def _():
        cut, seq = relayed.shape[0], out.shape[0]
        upper = pltpu.make_async_copy(relayed, out.at[pl.ds(0, cut), :], sem.at[0])
        lower = pltpu.make_async_copy(rest, out.at[pl.ds(cut, seq - cut), :], sem.at[1])
        upper.start()
        lower.start()
        upper.wait()
        lower.wait()

    for here, source in ((is_alone, alone), (is_direct, direct), (is_last, last)):

        @pl.when(here)
        def _():
            copy = pltpu.make_async_copy(source, out, sem.at[0])
            copy.start()
            copy.wait()


def call(kernel, count, heads, ins, out_shape, scratch, flops, moved, far_in=0, far_out=0):
    return pl.pallas_call(
        functools.partial(kernel, count, heads),
        out_shape=out_shape,
        in_specs=[any_spec() if far_in else vmem_spec()] * len(ins),
        out_specs=[any_spec() if far_out else vmem_spec()] * len(out_shape),
        scratch_shapes=scratch,
        compiler_params=pltpu.CompilerParams(vmem_limit_bytes=LIMIT),
        cost_estimate=pl.CostEstimate(flops=flops, bytes_accessed=moved, transcendentals=0),
    )(*ins)


def local(
    embedded, outbox, loss_grad, grad_outbox, stash_held, norm_gain, w_query, w_keyval, w_out
):
    sections = lax.axis_size("section")
    count = lax.axis_size("tensor")
    held, grads_held, stash_held = outbox[0], grad_outbox[0], stash_held[0]
    seq, width = held.shape
    model = width * count
    wq, wkv, wo = w_query[0], w_keyval[0], w_out[0]
    qcols, kvcols = wq.shape[1], wkv.shape[1]
    heads = qcols // HEAD
    shape = jax.ShapeDtypeStruct

    block = sections // 4
    high = sections - block

    def send(value, pairs):
        return lax.ppermute(value, "section", pairs)

    def early(t):
        return (t % block == 0) | (t > high)

    up = [(s, s + 1) for s in range(sections - 1)]
    soon = send(held, [(s, t) for s, t in up if early(t)])
    coming = send(grads_held, [(t, s) for s, t in up])
    fetched = send(stash_held, [(s, sections - 1 - s) for s in range(sections)])
    later = send(held, [(s, t) for s, t in up if not early(t)])
    evicted = send(held, [(s, sections - 2 - s) for s in range(high) if s != block - 1])
    alone = send(held, [(block - 1, sections - 1 - block)])
    cut = seq - seq // 16
    relayed = send(soon[:cut], [(s, sections - 1 - s) for s in range(high + 1, sections)])
    rest = send(held[cut:], [(s, sections - 2 - s) for s in range(high, sections - 1)])
    gains = gathered(norm_gain, "tensor")

    normed = pltpu.VMEM((seq, model), BF16)
    shares = [shape((seq, width), BF16)] * count
    proj = 2 * seq * model * (qcols + kvcols)
    out_flops = 2 * seq * model * qcols
    moved = 2 * model * (2 * qcols + kvcols)
    wq, wkv, wo = call(
        load_kernel, count, heads, [wq, wkv, wo],
        [shape(w.shape, w.dtype) for w in (wq, wkv, wo)],
        [pltpu.SemaphoreType.DMA((3,))], 0, 2 * moved, far_in=1,
    )
    bs = gathered(fetched, "tensor")

    def x_tests(place, sections):
        is_early = (place % block == 0) | (place > high)
        return place == 0, is_early & (place != 0), jnp.logical_not(is_early)

    def choose(tests, ins):
        (out,) = call(
            choose_kernel, count, tests, ins, [shape((seq, width), BF16)],
            [pltpu.SemaphoreType.DMA], 0, 4 * seq * width,
        )
        return out

    x_shard = choose(x_tests, [embedded, soon, later])
    xs = gathered(x_shard, "tensor")
    parts = call(
        forward_kernel, count, heads,
        [*xs, *gains, wq, wkv, wo], shares,
        [normed, pltpu.VMEM((seq, qcols), BF16)],
        proj + out_flops, moved,
    )
    g_shard = choose(lambda place, n: (place == n - 1, place != n - 1), [loss_grad, coming])
    gs = gathered(g_shard, "tensor")
    *terms, total, inv = call(
        backward_kernel, count, heads,
        [*gs, *bs, *gains, wq, wkv, wo],
        [*shares, shape((seq, HEAD), F32), shape((seq, HEAD), F32)],
        [
            normed,
            pltpu.VMEM((seq, qcols), BF16),
            pltpu.VMEM((heads, seq, seq), F32),
            pltpu.VMEM((seq, qcols), BF16),
        ],
        2 * proj + out_flops, moved,
    )
    mixed = reduced(parts, "tensor")
    section_out = (x_shard.astype(F32) + mixed).astype(BF16)
    own, *others = terms
    own, _ = lax.optimization_barrier((own, section_out))
    d_normed = reduced([own, *others], "tensor")
    total = sum(gathered(total, "tensor"))[:, :1]
    inv = inv[:, :1]
    scaled = d_normed * norm_gain.astype(F32)
    result = (
        g_shard.astype(F32) + inv * scaled - fetched.astype(F32) * inv**3 * (total / model)
    ).astype(BF16)
    last, _ = lax.optimization_barrier((embedded, (result, section_out)))
    (evicted,) = call(
        merge_kernel, count, block,
        [relayed, rest, alone, evicted, last], [shape((seq, width), BF16)],
        [pltpu.SemaphoreType.DMA((2,))], 0, 4 * seq * width, far_out=1,
    )
    return section_out[None], evicted[None], result[None]


def solution(mesh):
    return jax.shard_map(
        local,
        mesh=mesh,
        in_specs=(
            P(None, "tensor"),
            P("section", None, "tensor"),
            P(None, "tensor"),
            P("section", None, "tensor"),
            P("section", None, "tensor"),
            P("section", "tensor"),
            P("section", None, "tensor"),
            P("section", None, "tensor"),
            P("section", "tensor", None),
        ),
        out_specs=(
            P("section", None, "tensor"),
            P("section", None, "tensor"),
            P("section", None, "tensor"),
        ),
        check_vma=False,
    )
```
